128 devices in a mesh: seq: 8 (over z_lo, x), exp: 16 (over z_hi, y, core).
Axes of the slice: x: 4, y: 4, z: 4 (z_hi: 2, z_lo: 2; z = z_hi * 2 + z_lo), core: 2. Of those that a mesh axis runs over, the one named last changes fastest.
Arguments:
- tokens: bfloat16 [2, 98304, 1024], P(None, ('seq', 'exp')), may hold values from -60 to 60
- router: bfloat16 [1024, 128], replicated, may hold values from -0.25 to 0.25
- w_in: bfloat16 [32, 1024, 4096], P('exp', None, 'seq'), may hold values from -0.1875 to 0.1875
- w_out: bfloat16 [32, 4096, 1024], P('exp', 'seq'), may hold values from -0.09375 to 0.09375
- grad_out: bfloat16 [2, 98304, 1024], P(None, ('seq', 'exp')), may hold values from -6 to 6
Outputs:
- mixed: bfloat16 [2, 98304, 1024], P(None, ('seq', 'exp'))
- grad_tokens: bfloat16 [2, 98304, 1024], P(None, ('seq', 'exp'))
- grad_router: float32 [1024, 128], P(('seq', 'exp'))
- grad_w_in: bfloat16 [32, 1024, 4096], P('exp', None, 'seq')
- grad_w_out: bfloat16 [32, 4096, 1024], P('exp', 'seq')
The draws below stay inside these ranges and needn't reach their ends.
All inputs are finite; a program needn't handle non-finite values.
Results may differ from the reference program's by a relative error of at most 0.018.
Values may be sent and summed in bfloat16 or wider, within the bound.
No kernel may reach another device: no remote copies, remote signals or barrier semaphores. Data moves between devices by JAX's collectives and lax.ppermute only.
A program may use at most 128 MiB of HBM per device.

```python
import math
import jax
import jax.numpy as jnp
from jax import lax

D = 1024
FF = 4096
SLOTS = 4
CLIPS = 2
EXPERTS = 32
SLOT_COUNT = 128
TOKENS = 98304


def router_base(key):
    base = jax.random.normal(jax.random.fold_in(key, 7), (D, SLOT_COUNT), jnp.float32) / math.sqrt(D)
    return jnp.clip(base, -0.25, 0.25)


def draw_router(key, part):
    return router_base(key).astype(jnp.bfloat16)


def draw_tokens(key, part):
    values = jax.random.normal(jax.random.fold_in(key, 11), (CLIPS, TOKENS, D), jnp.float32)
    return jnp.clip(values, -6.0, 6.0).astype(jnp.bfloat16)


def block_levels(key, shape, split, least, top_value):
    def one(dim, blocks):
        steps = jax.random.uniform(jax.random.fold_in(jax.random.fold_in(key, 6), dim), (blocks,), jnp.float32, least / len(split), top_value / len(split))
        return jnp.repeat(jnp.exp(steps), shape[dim] // blocks).reshape((-1,) + (1,) * (len(shape) - dim - 1))

    loudness = one(*split[0])
    for cut in split[1:]:
        loudness = loudness * one(*cut)
    return loudness


def gaussian(stream_key, dims, spread, limit, split=(), kind=jnp.bfloat16):
    gain = block_levels(stream_key, dims, split, -0.22, 0.18) if split else 1.0
    array = jax.random.normal(stream_key, dims, jnp.float32) * spread * gain
    return jnp.minimum(jnp.maximum(array, -limit), limit).astype(kind)


def setup_inputs(seed: int = 0) -> dict:
    keys = jax.random.split(jax.random.key(seed), 6)
    return {
        "tokens": draw_tokens(jax.random.fold_in(keys[5], 71), 0),
        "router": draw_router(jax.random.fold_in(keys[5], 71), 0),
        "w_in": gaussian(keys[2], (EXPERTS, D, FF), D ** -0.5, 0.1875, ((0, 16), (2, 8))),
        "w_out": gaussian(keys[3], (EXPERTS, FF, D), FF ** -0.5, 0.09375, ((0, 16), (1, 8))),
        "grad_out": gaussian(keys[4], (CLIPS, TOKENS, D), 1.0, 6.0, ((1, 128),)),
    }


def reference(tokens, router, w_in, w_out, grad_out):
    width = tokens.shape[2]
    slot_total = router.shape[1]
    experts = w_in.shape[0]
    tokens_f = tokens.astype(jnp.float32)
    grad_f = grad_out.astype(jnp.float32)
    logits = jnp.dot(tokens.reshape(CLIPS * TOKENS, width).astype(jnp.float32), router.astype(jnp.float32), preferred_element_type=jnp.float32).reshape(CLIPS, TOKENS, slot_total)
    slot_peak = lax.optimization_barrier(jnp.max(logits, axis=1, keepdims=True))
    exp_terms = jnp.exp(logits - slot_peak)
    dispatch = exp_terms / lax.optimization_barrier(jnp.sum(exp_terms, axis=1, keepdims=True))
    dispatch_b = dispatch.astype(jnp.bfloat16)
    mixing = jax.nn.softmax(logits, axis=2)
    mixing_b = mixing.astype(jnp.bfloat16)
    slot_in = jnp.einsum('cts,ctd->scd', dispatch_b.astype(jnp.float32), tokens_f).astype(jnp.bfloat16)
    expert_rows = slot_in.reshape(experts, SLOTS * CLIPS, width)
    pre = jnp.einsum('erd,edh->erh', expert_rows.astype(jnp.float32), w_in.astype(jnp.float32))
    hidden = jax.nn.gelu(pre).astype(jnp.bfloat16)
    slot_out = jnp.einsum('erh,ehd->erd', hidden.astype(jnp.float32), w_out.astype(jnp.float32)).astype(jnp.bfloat16)
    slot_out = slot_out.reshape(slot_total, CLIPS, width)
    slot_out_f = slot_out.astype(jnp.float32)
    mixed = jnp.einsum('cts,scd->ctd', mixing_b.astype(jnp.float32), slot_out_f).astype(jnp.bfloat16)
    mixing_grad = jnp.einsum('ctd,scd->cts', grad_f, slot_out_f)
    slot_grad = jnp.einsum('cts,ctd->scd', mixing_b.astype(jnp.float32), grad_f).astype(jnp.bfloat16)
    grad_rows = slot_grad.reshape(experts, SLOTS * CLIPS, width).astype(jnp.float32)
    hidden_grad = jnp.einsum('erd,ehd->erh', grad_rows, w_out.astype(jnp.float32))
    pre_grad = jax.vjp(jax.nn.gelu, pre)[1](hidden_grad)[0].astype(jnp.bfloat16)
    pre_grad_f = pre_grad.astype(jnp.float32)
    grad_w_out = jnp.einsum('erh,erd->ehd', hidden.astype(jnp.float32), grad_rows).astype(jnp.bfloat16)
    grad_w_in = jnp.einsum('erd,erh->edh', expert_rows.astype(jnp.float32), pre_grad_f).astype(jnp.bfloat16)
    slot_in_grad = jnp.einsum('erh,edh->erd', pre_grad_f, w_in.astype(jnp.float32)).astype(jnp.bfloat16)
    slot_in_grad = slot_in_grad.reshape(slot_total, CLIPS, width).astype(jnp.float32)
    dispatch_grad = jnp.einsum('ctd,scd->cts', tokens_f, slot_in_grad)
    inner = lax.optimization_barrier(jnp.sum(dispatch * dispatch_grad, axis=1, keepdims=True))
    logit_grad = dispatch * (dispatch_grad - inner) + mixing * (mixing_grad - lax.optimization_barrier(jnp.sum(mixing * mixing_grad, axis=2, keepdims=True)))
    logit_b = logit_grad.astype(jnp.bfloat16)
    token_part = jnp.einsum('cts,scd->ctd', dispatch_b.astype(jnp.float32), slot_in_grad)
    router_part = jnp.dot(logit_b.reshape(CLIPS * TOKENS, slot_total).astype(jnp.float32), router.T.astype(jnp.float32), preferred_element_type=jnp.float32).reshape(CLIPS, TOKENS, width)
    grad_tokens = (token_part + router_part).astype(jnp.bfloat16)
    grad_router = jnp.einsum('ctd,cts->ds', tokens_f, logit_b.astype(jnp.float32))
    return (mixed, grad_tokens, grad_router, grad_w_in, grad_w_out)
```

```python
import functools

import jax
import jax.numpy as jnp
from jax import lax
from jax.experimental import pallas as pl
from jax.experimental.pallas import tpu as pltpu
from jax.sharding import Mesh
from jax.sharding import PartitionSpec as P

SEQ = ("seq_0", "seq_1")
EXP = ("exp_0", "exp_1", "exp_2")
CHIPS_EXP = ("exp_0", "exp_1")
CORE = "exp_2"
SEQ_EXP = SEQ + EXP

F32 = jnp.float32
BF16 = jnp.bfloat16
LANES = 128
GROUP = 8


def dot_nt(a, b):
    return lax.dot_general(a, b, (((1,), (1,)), ((), ())), preferred_element_type=F32)


def dot_nn(a, b):
    return lax.dot_general(a, b, (((1,), (0,)), ((), ())), preferred_element_type=F32)


def dot_tn(a, b):
    return lax.dot_general(a, b, (((0,), (0,)), ((), ())), preferred_element_type=F32)


def params(mib, grid_dims=0):
    kinds = ("arbitrary",) * grid_dims if grid_dims else None
    return pltpu.CompilerParams(vmem_limit_bytes=mib << 20, dimension_semantics=kinds)


def pieces(value, count):
    found = []
    for _ in range(count):
        part = value.astype(BF16).astype(F32)
        found.append(part)
        value = value - part
    return found


def packed(columns):
    rows = columns[0].shape[0]
    lane = lax.broadcasted_iota(jnp.int32, (rows, LANES), 1)
    tile = jnp.zeros((rows, LANES), F32)
    for k, column in enumerate(columns):
        tile = jnp.where(lane == k, column, tile)
    return tile


def mixing_of(logits_t):
    peak = jnp.max(logits_t, axis=0, keepdims=True)
    terms = jnp.exp(logits_t - peak)
    return terms / jnp.sum(terms, axis=0, keepdims=True)


def first_pass(tok_ref, router_ref, grad_ref, logits_ref, router_t_ref, send_ref, keep_ref, sums, stats):
    clip = pl.program_id(0)
    core = lax.axis_index(CORE)
    width = tok_ref.shape[2]

    @pl.when(clip == 0)
    def _():
        router_t_ref[...] = router_ref[...].T

    tok = tok_ref[0]
    logits_t = dot_nt(router_t_ref[...], tok)
    logits_ref[0] = logits_t
    peak = jnp.max(logits_t, axis=1, keepdims=True).astype(BF16).astype(F32)
    terms = jnp.exp(logits_t - peak)
    mass = jnp.sum(terms, axis=1, keepdims=True)
    sums[0] = dot_nn(terms.astype(BF16), tok)
    sums[1] = dot_nn(mixing_of(logits_t).astype(BF16), grad_ref[0])
    columns = [peak] + pieces(mass, 2)
    lane = lax.broadcasted_iota(jnp.int32, stats.shape, 1)
    for c in range(2):

        @pl.when(clip == c)
        def _(c=c):
            old = jnp.zeros(stats.shape, F32) if c == 0 else stats[...]
            for k, column in zip((c, 2 + 2 * c, 3 + 2 * c), columns):
                old = jnp.where(lane == k, column, old)
            stats[...] = old
            for q in range(send_ref.shape[0]):
                mine = pl.ds(pl.multiple_of((2 * q + core) * GROUP, GROUP), GROUP)
                other = pl.ds(pl.multiple_of((2 * q + 1 - core) * GROUP, GROUP), GROUP)
                for part in range(2):
                    at = pl.ds((2 * part + c) * width, width)
                    keep_ref[q, :, at] = sums[part, mine, :].astype(BF16)
                    send_ref[q, :, at] = sums[part, other, :].astype(BF16)
                if c == 1:
                    keep_ref[q, :, pl.ds(4 * width, LANES)] = stats[mine, :].astype(BF16)
                    send_ref[q, :, pl.ds(4 * width, LANES)] = stats[other, :].astype(BF16)


def run_first_pass(tokens, router, grad_out):
    clips, rows, width = tokens.shape
    slots = router.shape[1]
    row = 4 * width + LANES
    groups = slots // GROUP // 2
    whole = lambda *shape: pl.BlockSpec(shape, lambda c: (0,) * len(shape))
    per_clip = lambda *shape: pl.BlockSpec((1, *shape), lambda c: (c, 0, 0))
    return pl.pallas_call(
        first_pass,
        grid=(clips,),
        in_specs=[per_clip(rows, width), whole(width, slots), per_clip(rows, width)],
        out_specs=[
            per_clip(slots, rows),
            whole(slots, width),
            whole(groups, GROUP, row),
            whole(groups, GROUP, row),
        ],
        out_shape=[
            jax.ShapeDtypeStruct((clips, slots, rows), F32),
            jax.ShapeDtypeStruct((slots, width), BF16),
            jax.ShapeDtypeStruct((groups, GROUP, row), BF16),
            jax.ShapeDtypeStruct((groups, GROUP, row), BF16),
        ],
        scratch_shapes=[pltpu.VMEM((2, slots, width), F32), pltpu.VMEM((slots, LANES), F32)],
        compiler_params=params(28, 1),
        name="first_pass",
    )(tokens, router, grad_out)


def merged(blocks, width):
    tiles = [load(4 * width, LANES) for load in blocks]
    top = functools.reduce(jnp.maximum, tiles)
    scales = [jnp.exp(jnp.minimum(tile - top, 0.0)) for tile in tiles]
    inputs, grads, peaks, masses = [], [], [], []
    for c in range(2):
        peaks.append(top[:, c : c + 1])
        columns = [scale[:, c : c + 1] for scale in scales]
        masses.append(
            sum(col * (t[:, 2 + 2 * c : 3 + 2 * c] + t[:, 3 + 2 * c : 4 + 2 * c]) for col, t in zip(columns, tiles))
        )
        inputs.append(sum(col * load(c * width, width) for col, load in zip(columns, blocks)))
        grads.append(sum(load((2 + c) * width, width) for load in blocks))
    return inputs, grads, peaks, masses


def loader(ref, index):
    return lambda at, size: ref[index, :, pl.ds(at, size)].astype(F32)


def stat_tile(peaks, masses):
    return packed([peaks[0], peaks[1], *pieces(masses[0], 2), *pieces(masses[1], 2)])


def merge_cores(keep_ref, recv_ref, out_ref):
    width = (keep_ref.shape[2] - LANES) // 4
    for q in range(keep_ref.shape[0]):
        inputs, grads, peaks, masses = merged([loader(keep_ref, q), loader(recv_ref, q)], width)
        for k, value in enumerate(inputs + grads):
            out_ref[q, :, pl.ds(k * width, width)] = value.astype(BF16)
        out_ref[q, :, pl.ds(4 * width, LANES)] = stat_tile(peaks, masses).astype(BF16)


def merge_column(in_ref, out_ref):
    width = (in_ref.shape[2] - LANES) // 4
    blocks = [loader(in_ref, k) for k in range(in_ref.shape[0])]
    inputs, grads, peaks, masses = merged(blocks, width)
    for k, value in enumerate(inputs + grads):
        for q in range(out_ref.shape[0]):
            out_ref[q, :, pl.ds(k * width, width)] = value.astype(BF16)
    for q in range(out_ref.shape[0]):
        out_ref[q, :, pl.ds(4 * width, LANES)] = stat_tile(peaks, masses).astype(BF16)


GELU_A = 0.7978845608028654
GELU_B = 0.044715


def experts(in_ref, w_in_ref, w_out_ref, out_ref, rows_ref, grads_ref, hidden_ref, pre_grad_ref, slot_in_ref, stats_ref):
    width = w_in_ref.shape[1]
    count = w_in_ref.shape[0]
    blocks = [loader(in_ref, k) for k in range(in_ref.shape[0])]
    inputs, grads, peaks, masses = merged(blocks, width)
    slot_in = jnp.concatenate([value / mass for value, mass in zip(inputs, masses)], axis=0)
    slot_in_ref[...] = slot_in
    stats_ref[...] = packed([*peaks, *pieces(masses[0], 3), *pieces(masses[1], 3)])
    x = slot_in.astype(BF16)
    g = jnp.concatenate(grads, axis=0).astype(BF16)
    rows_ref[...] = x
    grads_ref[...] = g
    total = x.shape[0]
    hid = w_in_ref.shape[2]
    owner = lambda shape: lax.rem(lax.broadcasted_iota(jnp.int32, shape, 0), GROUP) // (GROUP // count)
    who = owner((total, hid))
    pre = jnp.zeros((total, hid), F32)
    hidden_grad = jnp.zeros((total, hid), F32)
    for e in range(count):
        pre = jnp.where(who == e, dot_nn(x, w_in_ref[e]), pre)
        hidden_grad = jnp.where(who == e, dot_nt(g, w_out_ref[e]), hidden_grad)
    inner = jnp.tanh(GELU_A * (pre + GELU_B * pre * pre * pre))
    hidden = 0.5 * pre * (1.0 + inner)
    slope = 0.5 * (1.0 + inner) + 0.5 * pre * (1.0 - inner * inner) * GELU_A * (1.0 + 3.0 * GELU_B * pre * pre)
    pre_grad = hidden_grad * slope
    hidden_ref[...] = hidden.astype(BF16)
    pre_grad_ref[...] = pre_grad.astype(BF16)
    out_part = jnp.zeros((total, width), F32)
    in_part = jnp.zeros((total, width), F32)
    for e in range(count):
        out_part += dot_nn(jnp.where(who == e, hidden, 0.0).astype(BF16), w_out_ref[e])
        in_part += dot_nt(jnp.where(who == e, pre_grad, 0.0).astype(BF16), w_in_ref[e])
    both = jnp.concatenate([out_part, in_part], axis=0).astype(BF16)
    for q in range(out_ref.shape[0]):
        out_ref[q] = both


def run_experts(sums, w_in, w_out):
    count, width, hid = w_in.shape
    peers = sums.shape[0]
    rows = 2 * GROUP
    return pl.pallas_call(
        experts,
        out_shape=[
            jax.ShapeDtypeStruct((peers, 2 * rows, width), BF16),
            jax.ShapeDtypeStruct((rows, width), BF16),
            jax.ShapeDtypeStruct((rows, width), BF16),
            jax.ShapeDtypeStruct((rows, hid), BF16),
            jax.ShapeDtypeStruct((rows, hid), BF16),
            jax.ShapeDtypeStruct((rows, width), F32),
            jax.ShapeDtypeStruct((GROUP, LANES), F32),
        ],
        compiler_params=params(16),
        name="experts",
    )(sums, w_in, w_out)


def weight_grads(rows_ref, grads_ref, hidden_ref, pre_grad_ref, w_in_grad_ref, w_out_grad_ref):
    e = pl.program_id(0)
    total, hid = hidden_ref.shape
    count = pl.num_programs(0)
    who = lax.rem(lax.broadcasted_iota(jnp.int32, (total, hid), 0), GROUP) // (GROUP // 2)
    mask = who == e
    hidden = jnp.where(mask, hidden_ref[...].astype(F32), 0.0).astype(BF16)
    pre_grad = jnp.where(mask, pre_grad_ref[...].astype(F32), 0.0).astype(BF16)
    w_out_grad_ref[0] = dot_tn(hidden, grads_ref[...]).astype(BF16)
    w_in_grad_ref[0] = dot_tn(rows_ref[...], pre_grad).astype(BF16)


def run_weight_grads(rows, grads, hidden, pre_grad, count):
    total, width = rows.shape
    hid = hidden.shape[1]
    whole = lambda *shape: pl.BlockSpec(shape, lambda e: (0,) * len(shape))
    return pl.pallas_call(
        weight_grads,
        grid=(count,),
        in_specs=[whole(total, width), whole(total, width), whole(total, hid), whole(total, hid)],
        out_specs=[
            pl.BlockSpec((1, width, hid), lambda e: (e, 0, 0)),
            pl.BlockSpec((1, hid, width), lambda e: (e, 0, 0)),
        ],
        out_shape=[
            jax.ShapeDtypeStruct((count, width, hid), BF16),
            jax.ShapeDtypeStruct((count, hid, width), BF16),
        ],
        compiler_params=params(16, 1),
        cost_estimate=pl.CostEstimate(
            flops=4 * count * total * width * hid, transcendentals=0, bytes_accessed=4 * count * width * hid
        ),
        name="weight_grads",
    )(rows, grads, hidden, pre_grad)


def slot_results(in_ref, slot_in_ref, stats_ref, out_ref):
    width = in_ref.shape[2]
    total = sum(in_ref[k].astype(F32) for k in range(in_ref.shape[0])).astype(BF16)
    back = total[2 * GROUP :].astype(F32)
    inner = jnp.sum(back * slot_in_ref[...], axis=1, keepdims=True)
    tile = stats_ref[...]
    lane = lax.broadcasted_iota(jnp.int32, tile.shape, 1)
    for c in range(2):
        for k, column in enumerate(pieces(inner[c * GROUP : (c + 1) * GROUP], 3)):
            tile = jnp.where(lane == 8 + 3 * c + k, column, tile)
    for q in range(out_ref.shape[0]):
        for k in range(4):
            out_ref[q, :, pl.ds(k * width, width)] = total[k * GROUP : (k + 1) * GROUP]
        out_ref[q, :, pl.ds(4 * width, LANES)] = tile.astype(BF16)


def second_pass(
    tok_ref, grad_ref, logits_ref, router_t_ref, mine_ref, other_ref,
    outs_ref, backs_ref, mix_ref, weights_ref, part_ref, stats, total,
):
    clip = pl.program_id(0)
    core = lax.axis_index(CORE)
    width = tok_ref.shape[2]
    slots = logits_ref.shape[1]

    @pl.when(clip == 0)
    def _():
        for way in range(2):

            @pl.when(core == way)
            def _(way=way):
                pair = (mine_ref, other_ref) if way == 0 else (other_ref, mine_ref)
                for q in range(mine_ref.shape[0]):
                    for half in range(2):
                        at = pl.ds((2 * q + half) * GROUP, GROUP)
                        for c in range(2):
                            outs_ref[c, at, :] = pair[half][q, :, pl.ds(c * width, width)]
                            backs_ref[c, at, :] = pair[half][q, :, pl.ds((2 + c) * width, width)]
                        stats[at, :] = pair[half][q, :, pl.ds(4 * width, LANES)].astype(F32)

        for c in range(2):
            backs_ref[c, pl.ds(slots, slots), :] = router_t_ref[...]
        total[...] = jnp.zeros_like(total)

    tile = stats[...]
    column = lambda k: jnp.where(clip == 0, tile[:, k[0] : k[0] + 1], tile[:, k[1] : k[1] + 1])
    peak = column((0, 1))
    mass = column((2, 5)) + column((3, 6)) + column((4, 7))
    inner = column((8, 11)) + column((9, 12)) + column((10, 13))
    logits_t = logits_ref[0]
    dispatch = jnp.exp(logits_t - peak) / mass
    mixing = mixing_of(logits_t)
    mix_ref[0] = mixing.astype(BF16)
    tok = tok_ref[0]
    dispatch_grad = dot_nt(backs_ref[clip, pl.ds(0, slots), :], tok)
    mixing_grad = dot_nt(outs_ref[clip], grad_ref[0])
    logit_grad = dispatch * (dispatch_grad - inner) + mixing * (
        mixing_grad - jnp.sum(mixing * mixing_grad, axis=0, keepdims=True)
    )
    logit_b = logit_grad.astype(BF16)
    weights_ref[0, pl.ds(0, slots), :] = dispatch.astype(BF16)
    weights_ref[0, pl.ds(slots, slots), :] = logit_b
    total[...] += dot_nn(logit_b, tok)

    @pl.when(clip == pl.num_programs(0) - 1)
    def _():
        part_ref[...] = total[...].T.astype(BF16)


def run_second_pass(tokens, grad_out, logits, router_t, mine, other):
    clips, rows, width = tokens.shape
    slots = router_t.shape[0]
    whole = lambda *shape: pl.BlockSpec(shape, lambda c: (0,) * len(shape))
    per_clip = lambda *shape: pl.BlockSpec((1, *shape), lambda c: (c, 0, 0))
    return pl.pallas_call(
        second_pass,
        grid=(clips,),
        in_specs=[
            per_clip(rows, width),
            per_clip(rows, width),
            per_clip(slots, rows),
            whole(slots, width),
            whole(*mine.shape),
            whole(*other.shape),
        ],
        out_specs=[
            whole(clips, slots, width),
            whole(clips, 2 * slots, width),
            per_clip(slots, rows),
            per_clip(2 * slots, rows),
            whole(width, slots),
        ],
        out_shape=[
            jax.ShapeDtypeStruct((clips, slots, width), BF16),
            jax.ShapeDtypeStruct((clips, 2 * slots, width), BF16),
            jax.ShapeDtypeStruct((clips, slots, rows), BF16),
            jax.ShapeDtypeStruct((clips, 2 * slots, rows), BF16),
            jax.ShapeDtypeStruct((width, slots), BF16),
        ],
        scratch_shapes=[pltpu.VMEM((slots, LANES), F32), pltpu.VMEM((slots, width), F32)],
        compiler_params=params(28, 1),
        name="second_pass",
    )(tokens, grad_out, logits, router_t, mine, other)


def token_outputs(mix_ref, weights_ref, outs_ref, backs_ref, mixed_ref, grad_tokens_ref):
    mixed_ref[0] = dot_tn(mix_ref[0], outs_ref[0]).astype(BF16)
    grad_tokens_ref[0] = dot_tn(weights_ref[0], backs_ref[0]).astype(BF16)


def run_token_outputs(mix, weights, outs, backs):
    clips, slots, rows = mix.shape
    width = outs.shape[2]
    block = 256
    out = pl.BlockSpec((1, block, width), lambda c, t: (c, t, 0))
    return pl.pallas_call(
        token_outputs,
        grid=(clips, rows // block),
        in_specs=[
            pl.BlockSpec((1, slots, block), lambda c, t: (c, 0, t)),
            pl.BlockSpec((1, 2 * slots, block), lambda c, t: (c, 0, t)),
            pl.BlockSpec((1, slots, width), lambda c, t: (c, 0, 0)),
            pl.BlockSpec((1, 2 * slots, width), lambda c, t: (c, 0, 0)),
        ],
        out_specs=[out, out],
        out_shape=[jax.ShapeDtypeStruct((clips, rows, width), BF16)] * 2,
        compiler_params=params(16, 2),
        cost_estimate=pl.CostEstimate(
            flops=6 * clips * rows * slots * width, transcendentals=0, bytes_accessed=6 * clips * rows * width
        ),
        name="token_outputs",
    )(mix, weights, outs, backs)


def add_up(in_ref, out_ref):
    out_ref[...] = jnp.sum(in_ref[...].astype(F32), axis=0)


def exchanged(array, axes):
    return lax.all_to_all(array, axes, split_axis=0, concat_axis=0, tiled=True)


def swapped(array):
    return lax.ppermute(array, CORE, [(0, 1), (1, 0)])


def on_device(tokens, router, w_in, w_out, grad_out):
    peers = lax.axis_size(SEQ)
    width = tokens.shape[2]
    row = 4 * width + LANES
    chips = lax.axis_size(CHIPS_EXP)
    logits, router_t, send, keep = run_first_pass(tokens, router, grad_out)
    recv = swapped(send)
    small = params(16)
    halves = pl.pallas_call(
        merge_cores, out_shape=jax.ShapeDtypeStruct((chips, GROUP, row), BF16), compiler_params=small, name="merge_cores"
    )(keep, recv)
    column = pl.pallas_call(
        merge_column, out_shape=jax.ShapeDtypeStruct((peers, GROUP, row), BF16), compiler_params=small, name="merge_column"
    )(exchanged(halves, CHIPS_EXP))
    parts, rows, grads, hidden, pre_grad, slot_in, stats = run_experts(exchanged(column, SEQ), w_in, w_out)
    arrived = exchanged(parts, SEQ)
    grad_w_in, grad_w_out = run_weight_grads(rows, grads, hidden, pre_grad, w_in.shape[0])
    results = pl.pallas_call(
        slot_results, out_shape=jax.ShapeDtypeStruct((chips, GROUP, row), BF16), compiler_params=small, name="slot_results"
    )(arrived, slot_in, stats)
    mine = exchanged(results, CHIPS_EXP)
    other = swapped(mine)
    outs, backs, mix, weights, part = run_second_pass(tokens, grad_out, logits, router_t, mine, other)
    devices = lax.axis_size(SEQ_EXP)
    arrived = exchanged(part.reshape(devices, width // devices, part.shape[1]), SEQ_EXP)
    mixed, grad_tokens = run_token_outputs(mix, weights, outs, backs)
    grad_router = pl.pallas_call(
        add_up, out_shape=jax.ShapeDtypeStruct(arrived.shape[1:], F32), compiler_params=small, name="add_up"
    )(arrived)
    return (mixed, grad_tokens, grad_router, grad_w_in, grad_w_out)


def solution(mesh):
    finer = Mesh(mesh.devices.reshape(2, 4, 2, 4, 2), SEQ_EXP)
    return jax.shard_map(
        on_device,
        mesh=finer,
        in_specs=(
            P(None, SEQ_EXP, None),
            P(),
            P(EXP, None, SEQ),
            P(EXP, SEQ, None),
            P(None, SEQ_EXP, None),
        ),
        out_specs=(
            P(None, SEQ_EXP, None),
            P(None, SEQ_EXP, None),
            P(SEQ_EXP, None),
            P(EXP, None, SEQ),
            P(EXP, SEQ, None),
        ),
        check_vma=False,
    )
```

```python
import functools

import jax
import jax.numpy as jnp
from jax import lax
from jax.experimental import pallas as pl
from jax.experimental.pallas import tpu as pltpu
from jax.sharding import Mesh
from jax.sharding import PartitionSpec as P

SEQ = ("seq_0", "seq_1")
EXP = ("exp_0", "exp_1", "exp_2")
CHIPS_EXP = ("exp_0", "exp_1")
CORE = "exp_2"
SEQ_EXP = SEQ + EXP

F32 = jnp.float32
BF16 = jnp.bfloat16
LANES = 128
GROUP = 8


def dot_nt(a, b):
    return lax.dot_general(a, b, (((1,), (1,)), ((), ())), preferred_element_type=F32)


def dot_nn(a, b):
    return lax.dot_general(a, b, (((1,), (0,)), ((), ())), preferred_element_type=F32)


def dot_tn(a, b):
    return lax.dot_general(a, b, (((0,), (0,)), ((), ())), preferred_element_type=F32)


def params(mib, grid_dims=0):
    kinds = ("arbitrary",) * grid_dims if grid_dims else None
    return pltpu.CompilerParams(vmem_limit_bytes=mib << 20, dimension_semantics=kinds)


def pieces(value, count):
    found = []
    for _ in range(count):
        part = value.astype(BF16).astype(F32)
        found.append(part)
        value = value - part
    return found


def packed(columns):
    rows = columns[0].shape[0]
    lane = lax.broadcasted_iota(jnp.int32, (rows, LANES), 1)
    tile = jnp.zeros((rows, LANES), F32)
    for k, column in enumerate(columns):
        tile = jnp.where(lane == k, column, tile)
    return tile


def mixing_of(logits_t):
    peak = jnp.max(logits_t, axis=0, keepdims=True)
    terms = jnp.exp(logits_t - peak)
    return terms / jnp.sum(terms, axis=0, keepdims=True)


def first_pass(
    tok_hbm, router_hbm, grad_hbm,
    tok_ref, grad_ref, router_t_ref, terms_ref, mixing_ref, mix_ref, stats_ref, keep_ref, send_ref,
    router_buf, router_f, sems,
):
    core = lax.axis_index(CORE)
    clips, rows, width = tok_ref.shape
    slots = router_t_ref.shape[0]
    half = slots // 2
    copies = [pltpu.make_async_copy(router_hbm, router_buf, sems.at[0])]
    for c in range(clips):
        copies.append(pltpu.make_async_copy(tok_hbm.at[c], tok_ref.at[c], sems.at[1 + c]))
    for c in range(clips):
        copies.append(pltpu.make_async_copy(grad_hbm.at[c], grad_ref.at[c], sems.at[1 + clips + c]))
    for copy in copies:
        copy.start()
    copies[0].wait()
    router_f[...] = router_buf[...].T.astype(F32)
    for k in range(slots // GROUP):
        place = k % (half // GROUP)
        side = core if k < half // GROUP else 1 - core
        at = pl.ds(pl.multiple_of((2 * place + side) * GROUP, GROUP), GROUP)
        router_t_ref[pl.ds(k * GROUP, GROUP), :] = router_f[at, :].astype(BF16)
    columns = [None] * 6
    for c in range(clips):
        copies[1 + c].wait()
        logits_t = dot_nt(router_t_ref[...], tok_ref[c])
        peak = jnp.max(logits_t, axis=1, keepdims=True).astype(BF16).astype(F32)
        terms = jnp.exp(logits_t - peak)
        terms_ref[c] = terms
        mass = jnp.sum(terms, axis=1, keepdims=True)
        columns[c] = peak
        columns[2 + 2 * c : 4 + 2 * c] = pieces(mass, 2)
        sums = dot_nn(terms.astype(BF16), tok_ref[c]).astype(BF16)
        mixing = mixing_of(logits_t)
        mixing_ref[c] = mixing
        mix_ref[c] = mixing.astype(BF16)
        for q in range(keep_ref.shape[0]):
            at = pl.ds(c * width, width)
            keep_ref[q, :, at] = sums[q * GROUP : (q + 1) * GROUP]
            send_ref[q, :, at] = sums[half + q * GROUP : half + (q + 1) * GROUP]
    stats = packed(columns)
    stats_ref[...] = stats
    stats = stats.astype(BF16)
    for q in range(keep_ref.shape[0]):
        at = pl.ds(4 * width, LANES)
        keep_ref[q, :, at] = stats[q * GROUP : (q + 1) * GROUP]
        send_ref[q, :, at] = stats[half + q * GROUP : half + (q + 1) * GROUP]
    for c in range(clips):
        copies[1 + clips + c].wait()
        sums = dot_nn(mix_ref[c], grad_ref[c]).astype(BF16)
        for q in range(keep_ref.shape[0]):
            at = pl.ds((2 + c) * width, width)
            keep_ref[q, :, at] = sums[q * GROUP : (q + 1) * GROUP]
            send_ref[q, :, at] = sums[half + q * GROUP : half + (q + 1) * GROUP]


VMEM = pl.BlockSpec(memory_space=pltpu.VMEM)
HBM = pl.BlockSpec(memory_space=pltpu.HBM)


def run_first_pass(tokens, router, grad_out):
    clips, rows, width = tokens.shape
    slots = router.shape[1]
    row = 4 * width + LANES
    groups = slots // GROUP // 2
    shapes = [
        (tokens.shape, BF16),
        (grad_out.shape, BF16),
        ((slots, width), BF16),
        ((clips, slots, rows), F32),
        ((clips, slots, rows), F32),
        ((clips, slots, rows), BF16),
        ((slots, LANES), F32),
        ((groups, GROUP, row), BF16),
        ((groups, GROUP, row), BF16),
    ]
    return pl.pallas_call(
        first_pass,
        in_specs=[HBM] * 3,
        out_specs=[VMEM] * len(shapes),
        out_shape=[jax.ShapeDtypeStruct(*shape) for shape in shapes],
        scratch_shapes=[
            pltpu.VMEM(router.shape, BF16),
            pltpu.VMEM((slots, width), F32),
            pltpu.SemaphoreType.DMA((1 + 2 * clips,)),
        ],
        compiler_params=params(28),
        name="first_pass",
    )(*(pltpu.with_memory_space_constraint(a, pltpu.HBM) for a in (tokens, router, grad_out)))


def merged(blocks, width):
    tiles = [load(4 * width, LANES) for load in blocks]
    top = functools.reduce(jnp.maximum, tiles)
    scales = [jnp.exp(jnp.minimum(tile - top, 0.0)) for tile in tiles]
    inputs, grads, peaks, masses = [], [], [], []
    for c in range(2):
        peaks.append(top[:, c : c + 1])
        columns = [scale[:, c : c + 1] for scale in scales]
        masses.append(
            sum(col * (t[:, 2 + 2 * c : 3 + 2 * c] + t[:, 3 + 2 * c : 4 + 2 * c]) for col, t in zip(columns, tiles))
        )
        inputs.append(sum(col * load(c * width, width) for col, load in zip(columns, blocks)))
        grads.append(sum(load((2 + c) * width, width) for load in blocks))
    return inputs, grads, peaks, masses


def loader(ref, index):
    return lambda at, size: ref[index, :, pl.ds(at, size)].astype(F32)


def stat_tile(peaks, masses):
    return packed([peaks[0], peaks[1], *pieces(masses[0], 2), *pieces(masses[1], 2)])


def merge_cores(keep_ref, recv_ref, out_ref):
    width = (keep_ref.shape[2] - LANES) // 4
    for q in range(keep_ref.shape[0]):
        inputs, grads, peaks, masses = merged([loader(keep_ref, q), loader(recv_ref, q)], width)
        for k, value in enumerate(inputs + grads):
            out_ref[q, :, pl.ds(k * width, width)] = value.astype(BF16)
        out_ref[q, :, pl.ds(4 * width, LANES)] = stat_tile(peaks, masses).astype(BF16)


def merge_column(in_ref, out_ref):
    width = (in_ref.shape[2] - LANES) // 4
    blocks = [loader(in_ref, k) for k in range(in_ref.shape[0])]
    inputs, grads, peaks, masses = merged(blocks, width)
    for k, value in enumerate(inputs + grads):
        for q in range(out_ref.shape[0]):
            out_ref[q, :, pl.ds(k * width, width)] = value.astype(BF16)
    for q in range(out_ref.shape[0]):
        out_ref[q, :, pl.ds(4 * width, LANES)] = stat_tile(peaks, masses).astype(BF16)


GELU_A = 0.7978845608028654
GELU_B = 0.044715


def experts(in_ref, w_in_ref, w_out_ref, out_ref, rows_ref, grads_ref, hidden_ref, pre_grad_ref, slot_in_ref, stats_ref):
    width = w_in_ref.shape[1]
    count = w_in_ref.shape[0]
    blocks = [loader(in_ref, k) for k in range(in_ref.shape[0])]
    inputs, grads, peaks, masses = merged(blocks, width)
    slot_in = jnp.concatenate([value / mass for value, mass in zip(inputs, masses)], axis=0)
    slot_in_ref[...] = slot_in
    stats_ref[...] = packed([*peaks, *pieces(masses[0], 3), *pieces(masses[1], 3)])
    x = slot_in.astype(BF16)
    g = jnp.concatenate(grads, axis=0).astype(BF16)
    rows_ref[...] = x
    grads_ref[...] = g
    total = x.shape[0]
    hid = w_in_ref.shape[2]
    owner = lambda shape: lax.rem(lax.broadcasted_iota(jnp.int32, shape, 0), GROUP) // (GROUP // count)
    who = owner((total, hid))
    pre = jnp.zeros((total, hid), F32)
    hidden_grad = jnp.zeros((total, hid), F32)
    for e in range(count):
        pre = jnp.where(who == e, dot_nn(x, w_in_ref[e]), pre)
        hidden_grad = jnp.where(who == e, dot_nt(g, w_out_ref[e]), hidden_grad)
    inner = jnp.tanh(GELU_A * (pre + GELU_B * pre * pre * pre))
    hidden = 0.5 * pre * (1.0 + inner)
    slope = 0.5 * (1.0 + inner) + 0.5 * pre * (1.0 - inner * inner) * GELU_A * (1.0 + 3.0 * GELU_B * pre * pre)
    pre_grad = hidden_grad * slope
    hidden_ref[...] = hidden.astype(BF16)
    pre_grad_ref[...] = pre_grad.astype(BF16)
    out_part = jnp.zeros((total, width), F32)
    in_part = jnp.zeros((total, width), F32)
    for e in range(count):
        out_part += dot_nn(jnp.where(who == e, hidden, 0.0).astype(BF16), w_out_ref[e])
        in_part += dot_nt(jnp.where(who == e, pre_grad, 0.0).astype(BF16), w_in_ref[e])
    both = jnp.concatenate([out_part, in_part], axis=0).astype(BF16)
    for q in range(out_ref.shape[0]):
        out_ref[q] = both


def run_experts(sums, w_in, w_out):
    count, width, hid = w_in.shape
    peers = sums.shape[0]
    rows = 2 * GROUP
    return pl.pallas_call(
        experts,
        out_shape=[
            jax.ShapeDtypeStruct((peers, 2 * rows, width), BF16),
            jax.ShapeDtypeStruct((rows, width), BF16),
            jax.ShapeDtypeStruct((rows, width), BF16),
            jax.ShapeDtypeStruct((rows, hid), BF16),
            jax.ShapeDtypeStruct((rows, hid), BF16),
            jax.ShapeDtypeStruct((rows, width), F32),
            jax.ShapeDtypeStruct((GROUP, LANES), F32),
        ],
        compiler_params=params(16),
        name="experts",
    )(sums, w_in, w_out)


def weight_grads(rows_ref, grads_ref, hidden_ref, pre_grad_ref, w_in_grad_ref, w_out_grad_ref):
    e = pl.program_id(0)
    total, hid = hidden_ref.shape
    count = pl.num_programs(0)
    who = lax.rem(lax.broadcasted_iota(jnp.int32, (total, hid), 0), GROUP) // (GROUP // 2)
    mask = who == e
    hidden = jnp.where(mask, hidden_ref[...].astype(F32), 0.0).astype(BF16)
    pre_grad = jnp.where(mask, pre_grad_ref[...].astype(F32), 0.0).astype(BF16)
    w_out_grad_ref[0] = dot_tn(hidden, grads_ref[...]).astype(BF16)
    w_in_grad_ref[0] = dot_tn(rows_ref[...], pre_grad).astype(BF16)


def run_weight_grads(rows, grads, hidden, pre_grad, count):
    total, width = rows.shape
    hid = hidden.shape[1]
    whole = lambda *shape: pl.BlockSpec(shape, lambda e: (0,) * len(shape))
    return pl.pallas_call(
        weight_grads,
        grid=(count,),
        in_specs=[whole(total, width), whole(total, width), whole(total, hid), whole(total, hid)],
        out_specs=[
            pl.BlockSpec((1, width, hid), lambda e: (e, 0, 0)),
            pl.BlockSpec((1, hid, width), lambda e: (e, 0, 0)),
        ],
        out_shape=[
            jax.ShapeDtypeStruct((count, width, hid), BF16),
            jax.ShapeDtypeStruct((count, hid, width), BF16),
        ],
        compiler_params=params(16, 1),
        cost_estimate=pl.CostEstimate(
            flops=4 * count * total * width * hid, transcendentals=0, bytes_accessed=4 * count * width * hid
        ),
        name="weight_grads",
    )(rows, grads, hidden, pre_grad)


def slot_results(in_ref, slot_in_ref, stats_ref, out_ref):
    width = in_ref.shape[2]
    total = sum(in_ref[k].astype(F32) for k in range(in_ref.shape[0])).astype(BF16)
    back = total[2 * GROUP :].astype(F32)
    inner = jnp.sum(back * slot_in_ref[...], axis=1, keepdims=True)
    tile = stats_ref[...]
    lane = lax.broadcasted_iota(jnp.int32, tile.shape, 1)
    for c in range(2):
        for k, column in enumerate(pieces(inner[c * GROUP : (c + 1) * GROUP], 3)):
            tile = jnp.where(lane == 8 + 3 * c + k, column, tile)
    for q in range(out_ref.shape[0]):
        for k in range(4):
            out_ref[q, :, pl.ds(k * width, width)] = total[k * GROUP : (k + 1) * GROUP]
        out_ref[q, :, pl.ds(4 * width, LANES)] = tile.astype(BF16)


def second_pass(
    tok_ref, grad_ref, terms_ref, mixing_ref, local_ref, router_t_ref, mine_ref, other_ref,
    outs_ref, backs_ref, weights_ref, part_ref, ordered,
):
    core = lax.axis_index(CORE)
    clips, rows, width = tok_ref.shape
    slots = router_t_ref.shape[0]
    half = slots // 2
    tiles = []
    for k, ref in enumerate((mine_ref, other_ref)):
        for q in range(ref.shape[0]):
            at = pl.ds(k * half + q * GROUP, GROUP)
            for c in range(clips):
                outs_ref[c, at, :] = ref[q, :, pl.ds(c * width, width)]
                backs_ref[c, at, :] = ref[q, :, pl.ds((2 + c) * width, width)]
            tiles.append(ref[q, :, pl.ds(4 * width, LANES)].astype(F32))
    tile = jnp.concatenate(tiles, axis=0)
    local = local_ref[...]
    column = lambda k: tile[:, k : k + 1]
    total = jnp.zeros((slots, width), F32)
    for c in range(clips):
        backs_ref[c, pl.ds(slots, slots), :] = router_t_ref[...]
        mass = column(2 + 3 * c) + column(3 + 3 * c) + column(4 + 3 * c)
        inner = column(8 + 3 * c) + column(9 + 3 * c) + column(10 + 3 * c)
        scale = jnp.exp(local[:, c : c + 1] - column(c)) / mass
        dispatch = terms_ref[c] * scale
        weights_ref[c, pl.ds(0, slots), :] = dispatch.astype(BF16)
        mixing = mixing_ref[c]
        dispatch_grad = dot_nt(backs_ref[c, pl.ds(0, slots), :], tok_ref[c])
        mixing_grad = dot_nt(outs_ref[c], grad_ref[c])
        logit_grad = dispatch * (dispatch_grad - inner) + mixing * (
            mixing_grad - jnp.sum(mixing * mixing_grad, axis=0, keepdims=True)
        )
        logit_b = logit_grad.astype(BF16)
        weights_ref[c, pl.ds(slots, slots), :] = logit_b
        total = total + dot_nn(logit_b, tok_ref[c])
    for k in range(slots // GROUP):
        place = k % (half // GROUP)
        side = core if k < half // GROUP else 1 - core
        at = pl.ds(pl.multiple_of((2 * place + side) * GROUP, GROUP), GROUP)
        ordered[at, :] = total[k * GROUP : (k + 1) * GROUP]
    part_ref[...] = ordered[...].T.astype(BF16)


def run_second_pass(tok, grad, terms, mixing, local, router_t, mine, other):
    clips, rows, width = tok.shape
    slots = router_t.shape[0]
    shapes = [(clips, slots, width), (clips, 2 * slots, width), (clips, 2 * slots, rows), (width, slots)]
    return pl.pallas_call(
        second_pass,
        in_specs=[VMEM] * 8,
        out_specs=[VMEM] * len(shapes),
        out_shape=[jax.ShapeDtypeStruct(shape, BF16) for shape in shapes],
        scratch_shapes=[pltpu.VMEM((slots, width), F32)],
        compiler_params=params(28),
        name="second_pass",
    )(tok, grad, terms, mixing, local, router_t, mine, other)


def token_outputs(mix_ref, weights_ref, outs_ref, backs_ref, mixed_ref, grad_tokens_ref):
    mixed_ref[0] = dot_tn(mix_ref[0], outs_ref[0]).astype(BF16)
    grad_tokens_ref[0] = dot_tn(weights_ref[0], backs_ref[0]).astype(BF16)


def run_token_outputs(mix, weights, outs, backs):
    clips, slots, rows = mix.shape
    width = outs.shape[2]
    block = 256
    out = pl.BlockSpec((1, block, width), lambda c, t: (c, t, 0))
    return pl.pallas_call(
        token_outputs,
        grid=(clips, rows // block),
        in_specs=[
            pl.BlockSpec((1, slots, block), lambda c, t: (c, 0, t)),
            pl.BlockSpec((1, 2 * slots, block), lambda c, t: (c, 0, t)),
            pl.BlockSpec((1, slots, width), lambda c, t: (c, 0, 0)),
            pl.BlockSpec((1, 2 * slots, width), lambda c, t: (c, 0, 0)),
        ],
        out_specs=[out, out],
        out_shape=[jax.ShapeDtypeStruct((clips, rows, width), BF16)] * 2,
        compiler_params=params(16, 2),
        cost_estimate=pl.CostEstimate(
            flops=6 * clips * rows * slots * width, transcendentals=0, bytes_accessed=6 * clips * rows * width
        ),
        name="token_outputs",
    )(mix, weights, outs, backs)


def add_up(in_ref, out_ref):
    rows, total = out_ref.shape[0], in_ref.shape[0]
    row = lax.broadcasted_iota(jnp.int32, (rows, total), 0)
    at = lax.broadcasted_iota(jnp.int32, (rows, total), 1)
    pick = jnp.where(lax.rem(at, rows) == row, 1.0, 0.0).astype(BF16)
    out_ref[...] = dot_nn(pick, in_ref[...])


def exchanged(array, axes):
    return lax.all_to_all(array, axes, split_axis=0, concat_axis=0, tiled=True)


def swapped(array):
    return lax.ppermute(array, CORE, [(0, 1), (1, 0)])


def on_device(tokens, router, w_in, w_out, grad_out):
    peers = lax.axis_size(SEQ)
    width = tokens.shape[2]
    row = 4 * width + LANES
    chips = lax.axis_size(CHIPS_EXP)
    tok, grad, router_t, terms, mixing, mix, local, keep, send = run_first_pass(tokens, router, grad_out)
    recv = swapped(send)
    small = params(16)
    halves = pl.pallas_call(
        merge_cores, out_shape=jax.ShapeDtypeStruct((chips, GROUP, row), BF16), compiler_params=small, name="merge_cores"
    )(keep, recv)
    column = pl.pallas_call(
        merge_column, out_shape=jax.ShapeDtypeStruct((peers, GROUP, row), BF16), compiler_params=small, name="merge_column"
    )(exchanged(halves, CHIPS_EXP))
    parts, rows, grads, hidden, pre_grad, slot_in, stats = run_experts(exchanged(column, SEQ), w_in, w_out)
    arrived = exchanged(parts, SEQ)
    grad_w_in, grad_w_out = run_weight_grads(rows, grads, hidden, pre_grad, w_in.shape[0])
    results = pl.pallas_call(
        slot_results, out_shape=jax.ShapeDtypeStruct((chips, GROUP, row), BF16), compiler_params=small, name="slot_results"
    )(arrived, slot_in, stats)
    mine = exchanged(results, CHIPS_EXP)
    other = swapped(mine)
    outs, backs, weights, part = run_second_pass(tok, grad, terms, mixing, local, router_t, mine, other)
    devices = lax.axis_size(SEQ_EXP)
    arrived = exchanged(part.reshape(devices, width // devices, part.shape[1]), SEQ_EXP)
    mixed, grad_tokens = run_token_outputs(mix, weights, outs, backs)
    grad_router = pl.pallas_call(
        add_up, out_shape=jax.ShapeDtypeStruct(arrived.shape[1:], F32), compiler_params=small, name="add_up"
    )(arrived.reshape(width, part.shape[1]))
    return (mixed, grad_tokens, grad_router, grad_w_in, grad_w_out)


def solution(mesh):
    finer = Mesh(mesh.devices.reshape(2, 4, 2, 4, 2), SEQ_EXP)
    return jax.shard_map(
        on_device,
        mesh=finer,
        in_specs=(
            P(None, SEQ_EXP, None),
            P(),
            P(EXP, None, SEQ),
            P(EXP, SEQ, None),
            P(None, SEQ_EXP, None),
        ),
        out_specs=(
            P(None, SEQ_EXP, None),
            P(None, SEQ_EXP, None),
            P(SEQ_EXP, None),
            P(EXP, None, SEQ),
            P(EXP, SEQ, None),
        ),
        check_vma=False,
    )
```

```python
import functools

import jax
import jax.numpy as jnp
from jax import lax
from jax.experimental import pallas as pl
from jax.experimental.pallas import tpu as pltpu
from jax.sharding import Mesh
from jax.sharding import PartitionSpec as P

SEQ = ("seq_0", "seq_1")
EXP = ("exp_0", "exp_1", "exp_2")
CHIPS_EXP = ("exp_0", "exp_1")
CORE = "exp_2"
SEQ_EXP = SEQ + EXP

F32 = jnp.float32
BF16 = jnp.bfloat16
LANES = 128
GROUP = 8


def dot_nt(a, b):
    return lax.dot_general(a, b, (((1,), (1,)), ((), ())), preferred_element_type=F32)


def dot_nn(a, b):
    return lax.dot_general(a, b, (((1,), (0,)), ((), ())), preferred_element_type=F32)


def dot_tn(a, b):
    return lax.dot_general(a, b, (((0,), (0,)), ((), ())), preferred_element_type=F32)


def params(mib, grid_dims=0):
    kinds = ("arbitrary",) * grid_dims if grid_dims else None
    return pltpu.CompilerParams(vmem_limit_bytes=mib << 20, dimension_semantics=kinds)


def pieces(value, count):
    found = []
    for _ in range(count):
        part = value.astype(BF16).astype(F32)
        found.append(part)
        value = value - part
    return found


def packed(columns):
    rows = columns[0].shape[0]
    lane = lax.broadcasted_iota(jnp.int32, (rows, LANES), 1)
    tile = jnp.zeros((rows, LANES), F32)
    for k, column in enumerate(columns):
        tile = jnp.where(lane == k, column, tile)
    return tile


def mixing_of(logits_t):
    peak = jnp.max(logits_t, axis=0, keepdims=True)
    terms = jnp.exp(logits_t - peak)
    return terms * (1.0 / jnp.sum(terms, axis=0, keepdims=True))


def first_pass(
    tok_hbm, router_hbm, grad_hbm,
    tok_ref, tok_t_ref, grad_ref, router_t_ref, terms_ref, mixing_ref, mix_ref, stats_ref, keep_ref, send_ref,
    router_buf, router_f, sems,
):
    core = lax.axis_index(CORE)
    clips, rows, width = tok_ref.shape
    slots = router_t_ref.shape[0]
    half = slots // 2
    copies = [pltpu.make_async_copy(router_hbm, router_buf, sems.at[0])]
    for c in range(clips):
        copies.append(pltpu.make_async_copy(tok_hbm.at[c], tok_ref.at[c], sems.at[1 + c]))
    for c in range(clips):
        copies.append(pltpu.make_async_copy(grad_hbm.at[c], grad_ref.at[c], sems.at[1 + clips + c]))
    for copy in copies:
        copy.start()
    copies[0].wait()
    router_f[...] = router_buf[...].T.astype(F32)
    for k in range(slots // GROUP):
        place = k % (half // GROUP)
        side = core if k < half // GROUP else 1 - core
        at = pl.ds(pl.multiple_of((2 * place + side) * GROUP, GROUP), GROUP)
        router_t_ref[pl.ds(k * GROUP, GROUP), :] = router_f[at, :].astype(BF16)
    columns = [None] * 6
    for c in range(clips):
        copies[1 + c].wait()
        tok_t_ref[:, pl.ds(c * rows, rows)] = tok_ref[c].T
    both = dot_nn(router_t_ref[...], tok_t_ref[...])
    for c in range(clips):
        logits_t = both[:, c * rows : (c + 1) * rows]
        peak = jnp.max(logits_t, axis=1, keepdims=True).astype(BF16).astype(F32)
        terms = jnp.exp(logits_t - peak)
        terms_ref[c] = terms
        mass = jnp.sum(terms, axis=1, keepdims=True)
        columns[c] = peak
        columns[2 + 2 * c : 4 + 2 * c] = pieces(mass, 2)
        sums = dot_nn(terms.astype(BF16), tok_ref[c]).astype(BF16)
        mixing = mixing_of(logits_t)
        mixing_ref[c] = mixing
        mix_ref[c] = mixing.astype(BF16)
        for q in range(keep_ref.shape[0]):
            at = pl.ds(c * width, width)
            keep_ref[q, :, at] = sums[q * GROUP : (q + 1) * GROUP]
            send_ref[q, :, at] = sums[half + q * GROUP : half + (q + 1) * GROUP]
    for c in range(clips):
        copies[1 + clips + c].wait()
    stats = packed(columns)
    stats_ref[...] = stats
    stats = stats.astype(BF16)
    for q in range(keep_ref.shape[0]):
        at = pl.ds(4 * width, LANES)
        keep_ref[q, :, at] = stats[q * GROUP : (q + 1) * GROUP]
        send_ref[q, :, at] = stats[half + q * GROUP : half + (q + 1) * GROUP]
    for c in range(clips):
        sums = dot_nn(mix_ref[c], grad_ref[c]).astype(BF16)
        for q in range(keep_ref.shape[0]):
            at = pl.ds((2 + c) * width, width)
            keep_ref[q, :, at] = sums[q * GROUP : (q + 1) * GROUP]
            send_ref[q, :, at] = sums[half + q * GROUP : half + (q + 1) * GROUP]


VMEM = pl.BlockSpec(memory_space=pltpu.VMEM)
HBM = pl.BlockSpec(memory_space=pltpu.HBM)


def run_first_pass(tokens, router, grad_out):
    clips, rows, width = tokens.shape
    slots = router.shape[1]
    row = 4 * width + LANES
    groups = slots // GROUP // 2
    shapes = [
        (tokens.shape, BF16),
        ((width, clips * rows), BF16),
        (grad_out.shape, BF16),
        ((slots, width), BF16),
        ((clips, slots, rows), F32),
        ((clips, slots, rows), F32),
        ((clips, slots, rows), BF16),
        ((slots, LANES), F32),
        ((groups, GROUP, row), BF16),
        ((groups, GROUP, row), BF16),
    ]
    return pl.pallas_call(
        first_pass,
        in_specs=[HBM] * 3,
        out_specs=[VMEM] * len(shapes),
        out_shape=[jax.ShapeDtypeStruct(*shape) for shape in shapes],
        scratch_shapes=[
            pltpu.VMEM(router.shape, BF16),
            pltpu.VMEM((slots, width), F32),
            pltpu.SemaphoreType.DMA((1 + 2 * clips,)),
        ],
        compiler_params=params(28),
        name="first_pass",
    )(*(pltpu.with_memory_space_constraint(a, pltpu.HBM) for a in (tokens, router, grad_out)))


def merged(blocks, width):
    tiles = [load(4 * width, LANES) for load in blocks]
    top = functools.reduce(jnp.maximum, tiles)
    scales = [jnp.exp(jnp.minimum(tile - top, 0.0)) for tile in tiles]
    inputs, grads, peaks, masses = [], [], [], []
    for c in range(2):
        peaks.append(top[:, c : c + 1])
        columns = [scale[:, c : c + 1] for scale in scales]
        masses.append(
            sum(col * (t[:, 2 + 2 * c : 3 + 2 * c] + t[:, 3 + 2 * c : 4 + 2 * c]) for col, t in zip(columns, tiles))
        )
        inputs.append(sum(col * load(c * width, width) for col, load in zip(columns, blocks)))
        grads.append(sum(load((2 + c) * width, width) for load in blocks))
    return inputs, grads, peaks, masses


def loader(ref, index):
    return lambda at, size: ref[index, :, pl.ds(at, size)].astype(F32)


def stat_tile(peaks, masses):
    return packed([peaks[0], peaks[1], *pieces(masses[0], 2), *pieces(masses[1], 2)])


def merge_cores(keep_ref, recv_ref, out_ref):
    width = (keep_ref.shape[2] - LANES) // 4
    for q in range(keep_ref.shape[0]):
        inputs, grads, peaks, masses = merged([loader(keep_ref, q), loader(recv_ref, q)], width)
        for k, value in enumerate(inputs + grads):
            out_ref[q, :, pl.ds(k * width, width)] = value.astype(BF16)
        out_ref[q, :, pl.ds(4 * width, LANES)] = stat_tile(peaks, masses).astype(BF16)


def merge_column(in_ref, out_ref):
    width = (in_ref.shape[2] - LANES) // 4
    blocks = [loader(in_ref, k) for k in range(in_ref.shape[0])]
    inputs, grads, peaks, masses = merged(blocks, width)
    for k, value in enumerate(inputs + grads):
        for q in range(out_ref.shape[0]):
            out_ref[q, :, pl.ds(k * width, width)] = value.astype(BF16)
    for q in range(out_ref.shape[0]):
        out_ref[q, :, pl.ds(4 * width, LANES)] = stat_tile(peaks, masses).astype(BF16)


GELU_A = 0.7978845608028654
GELU_B = 0.044715


def experts(in_ref, w_in_ref, w_out_ref, out_ref, rows_ref, grads_ref, hidden_ref, pre_grad_ref, slot_in_ref, stats_ref):
    width = w_in_ref.shape[1]
    count = w_in_ref.shape[0]
    blocks = [loader(in_ref, k) for k in range(in_ref.shape[0])]
    inputs, grads, peaks, masses = merged(blocks, width)
    slot_in = jnp.concatenate([value / mass for value, mass in zip(inputs, masses)], axis=0)
    slot_in_ref[...] = slot_in
    stats_ref[...] = packed([*peaks, *pieces(masses[0], 3), *pieces(masses[1], 3)])
    x = slot_in.astype(BF16)
    g = jnp.concatenate(grads, axis=0).astype(BF16)
    rows_ref[...] = x
    grads_ref[...] = g
    total = x.shape[0]
    hid = w_in_ref.shape[2]
    owner = lambda shape: lax.rem(lax.broadcasted_iota(jnp.int32, shape, 0), GROUP) // (GROUP // count)
    who = owner((total, hid))
    pre = jnp.zeros((total, hid), F32)
    hidden_grad = jnp.zeros((total, hid), F32)
    for e in range(count):
        pre = jnp.where(who == e, dot_nn(x, w_in_ref[e]), pre)
        hidden_grad = jnp.where(who == e, dot_nt(g, w_out_ref[e]), hidden_grad)
    inner = jnp.tanh(GELU_A * (pre + GELU_B * pre * pre * pre))
    hidden = 0.5 * pre * (1.0 + inner)
    slope = 0.5 * (1.0 + inner) + 0.5 * pre * (1.0 - inner * inner) * GELU_A * (1.0 + 3.0 * GELU_B * pre * pre)
    pre_grad = hidden_grad * slope
    hidden_ref[...] = hidden.astype(BF16)
    pre_grad_ref[...] = pre_grad.astype(BF16)
    out_part = jnp.zeros((total, width), F32)
    in_part = jnp.zeros((total, width), F32)
    for e in range(count):
        out_part += dot_nn(jnp.where(who == e, hidden, 0.0).astype(BF16), w_out_ref[e])
        in_part += dot_nt(jnp.where(who == e, pre_grad, 0.0).astype(BF16), w_in_ref[e])
    both = jnp.concatenate([out_part, in_part], axis=0).astype(BF16)
    for q in range(out_ref.shape[0]):
        out_ref[q] = both


def run_experts(sums, w_in, w_out):
    count, width, hid = w_in.shape
    peers = sums.shape[0]
    rows = 2 * GROUP
    return pl.pallas_call(
        experts,
        out_shape=[
            jax.ShapeDtypeStruct((peers, 2 * rows, width), BF16),
            jax.ShapeDtypeStruct((rows, width), BF16),
            jax.ShapeDtypeStruct((rows, width), BF16),
            jax.ShapeDtypeStruct((rows, hid), BF16),
            jax.ShapeDtypeStruct((rows, hid), BF16),
            jax.ShapeDtypeStruct((rows, width), F32),
            jax.ShapeDtypeStruct((GROUP, LANES), F32),
        ],
        compiler_params=params(16),
        name="experts",
    )(sums, w_in, w_out)


def weight_grads(rows_ref, grads_ref, hidden_ref, pre_grad_ref, w_in_grad_ref, w_out_grad_ref):
    e = pl.program_id(0)
    total, hid = hidden_ref.shape
    count = pl.num_programs(0)
    who = lax.rem(lax.broadcasted_iota(jnp.int32, (total, hid), 0), GROUP) // (GROUP // 2)
    mask = who == e
    hidden = jnp.where(mask, hidden_ref[...].astype(F32), 0.0).astype(BF16)
    pre_grad = jnp.where(mask, pre_grad_ref[...].astype(F32), 0.0).astype(BF16)
    w_out_grad_ref[0] = dot_tn(hidden, grads_ref[...]).astype(BF16)
    w_in_grad_ref[0] = dot_tn(rows_ref[...], pre_grad).astype(BF16)


def run_weight_grads(rows, grads, hidden, pre_grad, count):
    total, width = rows.shape
    hid = hidden.shape[1]
    whole = lambda *shape: pl.BlockSpec(shape, lambda e: (0,) * len(shape))
    return pl.pallas_call(
        weight_grads,
        grid=(count,),
        in_specs=[whole(total, width), whole(total, width), whole(total, hid), whole(total, hid)],
        out_specs=[
            pl.BlockSpec((1, width, hid), lambda e: (e, 0, 0)),
            pl.BlockSpec((1, hid, width), lambda e: (e, 0, 0)),
        ],
        out_shape=[
            jax.ShapeDtypeStruct((count, width, hid), BF16),
            jax.ShapeDtypeStruct((count, hid, width), BF16),
        ],
        compiler_params=params(16, 1),
        cost_estimate=pl.CostEstimate(
            flops=4 * count * total * width * hid, transcendentals=0, bytes_accessed=4 * count * width * hid
        ),
        name="weight_grads",
    )(rows, grads, hidden, pre_grad)


def slot_results(in_ref, slot_in_ref, stats_ref, out_ref):
    width = in_ref.shape[2]
    total = sum(in_ref[k].astype(F32) for k in range(in_ref.shape[0])).astype(BF16)
    back = total[2 * GROUP :].astype(F32)
    inner = jnp.sum(back * slot_in_ref[...], axis=1, keepdims=True)
    tile = stats_ref[...]
    lane = lax.broadcasted_iota(jnp.int32, tile.shape, 1)
    for c in range(2):
        for k, column in enumerate(pieces(inner[c * GROUP : (c + 1) * GROUP], 3)):
            tile = jnp.where(lane == 8 + 3 * c + k, column, tile)
    for q in range(out_ref.shape[0]):
        for k in range(4):
            out_ref[q, :, pl.ds(k * width, width)] = total[k * GROUP : (k + 1) * GROUP]
        out_ref[q, :, pl.ds(4 * width, LANES)] = tile.astype(BF16)


def second_pass(
    tok_ref, tok_t_ref, grad_ref, terms_ref, mixing_ref, local_ref, router_t_ref, mine_ref, other_ref,
    outs_ref, backs_ref, weights_ref, part_ref, ordered,
):
    core = lax.axis_index(CORE)
    clips, rows, width = tok_ref.shape
    slots = router_t_ref.shape[0]
    half = slots // 2
    tiles = []
    for k, ref in enumerate((mine_ref, other_ref)):
        for q in range(ref.shape[0]):
            at = pl.ds(k * half + q * GROUP, GROUP)
            for c in range(clips):
                outs_ref[c, at, :] = ref[q, :, pl.ds(c * width, width)]
                backs_ref[c, at, :] = ref[q, :, pl.ds((2 + c) * width, width)]
            tiles.append(ref[q, :, pl.ds(4 * width, LANES)].astype(F32))
    tile = jnp.concatenate(tiles, axis=0)
    local = local_ref[...]
    column = lambda k: tile[:, k : k + 1]
    total = jnp.zeros((slots, width), F32)
    for c in range(clips):
        backs_ref[c, pl.ds(slots, slots), :] = router_t_ref[...]
        mass = column(2 + 3 * c) + column(3 + 3 * c) + column(4 + 3 * c)
        inner = column(8 + 3 * c) + column(9 + 3 * c) + column(10 + 3 * c)
        scale = jnp.exp(local[:, c : c + 1] - column(c)) / mass
        dispatch = terms_ref[c] * scale
        weights_ref[c, pl.ds(0, slots), :] = dispatch.astype(BF16)
        mixing = mixing_ref[c]
        dispatch_grad = dot_nn(backs_ref[c, pl.ds(0, slots), :], tok_t_ref[:, pl.ds(c * rows, rows)])
        mixing_grad = dot_nt(outs_ref[c], grad_ref[c])
        logit_grad = dispatch * (dispatch_grad - inner) + mixing * (
            mixing_grad - jnp.sum(mixing * mixing_grad, axis=0, keepdims=True)
        )
        logit_b = logit_grad.astype(BF16)
        weights_ref[c, pl.ds(slots, slots), :] = logit_b
        total = total + dot_nn(logit_b, tok_ref[c])
    for k in range(slots // GROUP):
        place = k % (half // GROUP)
        side = core if k < half // GROUP else 1 - core
        at = pl.ds(pl.multiple_of((2 * place + side) * GROUP, GROUP), GROUP)
        ordered[at, :] = total[k * GROUP : (k + 1) * GROUP]
    part_ref[...] = ordered[...].T.astype(BF16)


def run_second_pass(tok, tok_t, grad, terms, mixing, local, router_t, mine, other):
    clips, rows, width = tok.shape
    slots = router_t.shape[0]
    shapes = [(clips, slots, width), (clips, 2 * slots, width), (clips, 2 * slots, rows), (width, slots)]
    return pl.pallas_call(
        second_pass,
        in_specs=[VMEM] * 9,
        out_specs=[VMEM] * len(shapes),
        out_shape=[jax.ShapeDtypeStruct(shape, BF16) for shape in shapes],
        scratch_shapes=[pltpu.VMEM((slots, width), F32)],
        compiler_params=params(28),
        name="second_pass",
    )(tok, tok_t, grad, terms, mixing, local, router_t, mine, other)


def token_outputs(mix_ref, weights_ref, outs_ref, backs_ref, mixed_ref, grad_tokens_ref):
    mixed_ref[0] = dot_tn(mix_ref[0], outs_ref[0]).astype(BF16)
    grad_tokens_ref[0] = dot_tn(weights_ref[0], backs_ref[0]).astype(BF16)


def run_token_outputs(mix, weights, outs, backs):
    clips, slots, rows = mix.shape
    width = outs.shape[2]
    block = 256
    out = pl.BlockSpec((1, block, width), lambda c, t: (c, t, 0))
    return pl.pallas_call(
        token_outputs,
        grid=(clips, rows // block),
        in_specs=[
            pl.BlockSpec((1, slots, block), lambda c, t: (c, 0, t)),
            pl.BlockSpec((1, 2 * slots, block), lambda c, t: (c, 0, t)),
            pl.BlockSpec((1, slots, width), lambda c, t: (c, 0, 0)),
            pl.BlockSpec((1, 2 * slots, width), lambda c, t: (c, 0, 0)),
        ],
        out_specs=[out, out],
        out_shape=[jax.ShapeDtypeStruct((clips, rows, width), BF16)] * 2,
        compiler_params=params(16, 2),
        cost_estimate=pl.CostEstimate(
            flops=6 * clips * rows * slots * width, transcendentals=0, bytes_accessed=6 * clips * rows * width
        ),
        name="token_outputs",
    )(mix, weights, outs, backs)


def add_up(in_ref, out_ref):
    rows, total = out_ref.shape[0], in_ref.shape[0]
    row = lax.broadcasted_iota(jnp.int32, (rows, total), 0)
    at = lax.broadcasted_iota(jnp.int32, (rows, total), 1)
    pick = jnp.where(lax.rem(at, rows) == row, 1.0, 0.0).astype(BF16)
    out_ref[...] = dot_nn(pick, in_ref[...])


def exchanged(array, axes):
    return lax.all_to_all(array, axes, split_axis=0, concat_axis=0, tiled=True)


def swapped(array):
    return lax.ppermute(array, CORE, [(0, 1), (1, 0)])


def on_device(tokens, router, w_in, w_out, grad_out):
    peers = lax.axis_size(SEQ)
    width = tokens.shape[2]
    row = 4 * width + LANES
    chips = lax.axis_size(CHIPS_EXP)
    tok, tok_t, grad, router_t, terms, mixing, mix, local, keep, send = run_first_pass(tokens, router, grad_out)
    recv = swapped(send)
    small = params(16)
    halves = pl.pallas_call(
        merge_cores, out_shape=jax.ShapeDtypeStruct((chips, GROUP, row), BF16), compiler_params=small, name="merge_cores"
    )(keep, recv)
    column = pl.pallas_call(
        merge_column, out_shape=jax.ShapeDtypeStruct((peers, GROUP, row), BF16), compiler_params=small, name="merge_column"
    )(exchanged(halves, CHIPS_EXP))
    parts, rows, grads, hidden, pre_grad, slot_in, stats = run_experts(exchanged(column, SEQ), w_in, w_out)
    arrived = exchanged(parts, SEQ)
    grad_w_in, grad_w_out = run_weight_grads(rows, grads, hidden, pre_grad, w_in.shape[0])
    results = pl.pallas_call(
        slot_results, out_shape=jax.ShapeDtypeStruct((chips, GROUP, row), BF16), compiler_params=small, name="slot_results"
    )(arrived, slot_in, stats)
    mine = exchanged(results, CHIPS_EXP)
    other = swapped(mine)
    outs, backs, weights, part = run_second_pass(tok, tok_t, grad, terms, mixing, local, router_t, mine, other)
    devices = lax.axis_size(SEQ_EXP)
    arrived = exchanged(part.reshape(devices, width // devices, part.shape[1]), SEQ_EXP)
    mixed, grad_tokens = run_token_outputs(mix, weights, outs, backs)
    grad_router = pl.pallas_call(
        add_up, out_shape=jax.ShapeDtypeStruct(arrived.shape[1:], F32), compiler_params=small, name="add_up"
    )(arrived.reshape(width, part.shape[1]))
    return (mixed, grad_tokens, grad_router, grad_w_in, grad_w_out)


def solution(mesh):
    finer = Mesh(mesh.devices.reshape(2, 4, 2, 4, 2), SEQ_EXP)
    return jax.shard_map(
        on_device,
        mesh=finer,
        in_specs=(
            P(None, SEQ_EXP, None),
            P(),
            P(EXP, None, SEQ),
            P(EXP, SEQ, None),
            P(None, SEQ_EXP, None),
        ),
        out_specs=(
            P(None, SEQ_EXP, None),
            P(None, SEQ_EXP, None),
            P(SEQ_EXP, None),
            P(EXP, None, SEQ),
            P(EXP, SEQ, None),
        ),
        check_vma=False,
    )
```

```python
import functools

import jax
import jax.numpy as jnp
from jax import lax
from jax.experimental import pallas as pl
from jax.experimental.pallas import tpu as pltpu
from jax.sharding import Mesh
from jax.sharding import PartitionSpec as P

SEQ = ("seq_0", "seq_1")
EXP = ("exp_0", "exp_1", "exp_2")
CHIPS_EXP = ("exp_0", "exp_1")
CORE = "exp_2"
SEQ_EXP = SEQ + EXP

F32 = jnp.float32
BF16 = jnp.bfloat16
LANES = 128
GROUP = 8


def dot_nt(a, b):
    return lax.dot_general(a, b, (((1,), (1,)), ((), ())), preferred_element_type=F32)


def dot_nn(a, b):
    return lax.dot_general(a, b, (((1,), (0,)), ((), ())), preferred_element_type=F32)


def dot_tn(a, b):
    return lax.dot_general(a, b, (((0,), (0,)), ((), ())), preferred_element_type=F32)


def params(mib, grid_dims=0):
    kinds = ("arbitrary",) * grid_dims if grid_dims else None
    return pltpu.CompilerParams(vmem_limit_bytes=mib << 20, dimension_semantics=kinds)


def pieces(value, count):
    found = []
    for _ in range(count):
        part = value.astype(BF16).astype(F32)
        found.append(part)
        value = value - part
    return found


def packed(columns):
    rows = columns[0].shape[0]
    lane = lax.broadcasted_iota(jnp.int32, (rows, LANES), 1)
    tile = jnp.zeros((rows, LANES), F32)
    for k, column in enumerate(columns):
        tile = jnp.where(lane == k, column, tile)
    return tile


def mixing_of(logits_t):
    peak = jnp.max(logits_t, axis=0, keepdims=True)
    terms = jnp.exp(logits_t - peak)
    return terms * (1.0 / jnp.sum(terms, axis=0, keepdims=True))


def first_pass(
    tok_hbm, router_hbm, grad_hbm,
    tok_ref, tok_t_ref, grad_ref, router_t_ref, terms_ref, mixing_ref, mix_ref, stats_ref, keep_ref, send_ref,
    router_buf, router_f, sems,
):
    core = lax.axis_index(CORE)
    clips, rows, width = tok_ref.shape
    slots = router_t_ref.shape[0]
    half = slots // 2
    copies = [pltpu.make_async_copy(router_hbm, router_buf, sems.at[0])]
    for c in range(clips):
        copies.append(pltpu.make_async_copy(tok_hbm.at[c], tok_ref.at[c], sems.at[1 + c]))
    for c in range(clips):
        copies.append(pltpu.make_async_copy(grad_hbm.at[c], grad_ref.at[c], sems.at[1 + clips + c]))
    for copy in copies:
        copy.start()
    copies[0].wait()
    router_f[...] = router_buf[...].T.astype(F32)
    for k in range(slots // GROUP):
        place = k % (half // GROUP)
        side = core if k < half // GROUP else 1 - core
        at = pl.ds(pl.multiple_of((2 * place + side) * GROUP, GROUP), GROUP)
        router_t_ref[pl.ds(k * GROUP, GROUP), :] = router_f[at, :].astype(BF16)
    columns = [None] * 6
    for c in range(clips):
        copies[1 + c].wait()
        tok_t_ref[:, pl.ds(c * rows, rows)] = tok_ref[c].T
    both = dot_nn(router_t_ref[...], tok_t_ref[...])
    for c in range(clips):
        logits_t = both[:, c * rows : (c + 1) * rows]
        peak = jnp.max(logits_t, axis=1, keepdims=True).astype(BF16).astype(F32)
        terms = jnp.exp(logits_t - peak)
        terms_ref[c] = terms
        mass = jnp.sum(terms, axis=1, keepdims=True)
        columns[c] = peak
        columns[2 + 2 * c : 4 + 2 * c] = pieces(mass, 2)
        sums = dot_nn(terms.astype(BF16), tok_ref[c]).astype(BF16)
        mixing = mixing_of(logits_t)
        mixing_ref[c] = mixing
        mix_ref[c] = mixing.astype(BF16)
        for q in range(keep_ref.shape[0]):
            at = pl.ds(c * width, width)
            keep_ref[q, :, at] = sums[q * GROUP : (q + 1) * GROUP]
            send_ref[q, :, at] = sums[half + q * GROUP : half + (q + 1) * GROUP]
    for c in range(clips):
        copies[1 + clips + c].wait()
    stats = packed(columns)
    stats_ref[...] = stats
    stats = stats.astype(BF16)
    for q in range(keep_ref.shape[0]):
        at = pl.ds(4 * width, LANES)
        keep_ref[q, :, at] = stats[q * GROUP : (q + 1) * GROUP]
        send_ref[q, :, at] = stats[half + q * GROUP : half + (q + 1) * GROUP]
    for c in range(clips):
        sums = dot_nn(mix_ref[c], grad_ref[c]).astype(BF16)
        for q in range(keep_ref.shape[0]):
            at = pl.ds((2 + c) * width, width)
            keep_ref[q, :, at] = sums[q * GROUP : (q + 1) * GROUP]
            send_ref[q, :, at] = sums[half + q * GROUP : half + (q + 1) * GROUP]


VMEM = pl.BlockSpec(memory_space=pltpu.VMEM)
HBM = pl.BlockSpec(memory_space=pltpu.HBM)


def run_first_pass(tokens, router, grad_out):
    clips, rows, width = tokens.shape
    slots = router.shape[1]
    row = 4 * width + LANES
    groups = slots // GROUP // 2
    shapes = [
        (tokens.shape, BF16),
        ((width, clips * rows), BF16),
        (grad_out.shape, BF16),
        ((slots, width), BF16),
        ((clips, slots, rows), F32),
        ((clips, slots, rows), F32),
        ((clips, slots, rows), BF16),
        ((slots, LANES), F32),
        ((groups, GROUP, row), BF16),
        ((groups, GROUP, row), BF16),
    ]
    return pl.pallas_call(
        first_pass,
        in_specs=[HBM] * 3,
        out_specs=[VMEM] * len(shapes),
        out_shape=[jax.ShapeDtypeStruct(*shape) for shape in shapes],
        scratch_shapes=[
            pltpu.VMEM(router.shape, BF16),
            pltpu.VMEM((slots, width), F32),
            pltpu.SemaphoreType.DMA((1 + 2 * clips,)),
        ],
        compiler_params=params(28),
        name="first_pass",
    )(*(pltpu.with_memory_space_constraint(a, pltpu.HBM) for a in (tokens, router, grad_out)))


def merged(blocks, width):
    tiles = [load(4 * width, LANES) for load in blocks]
    top = functools.reduce(jnp.maximum, tiles)
    scales = [jnp.exp(jnp.minimum(tile - top, 0.0)) for tile in tiles]
    inputs, grads, peaks, masses = [], [], [], []
    for c in range(2):
        peaks.append(top[:, c : c + 1])
        columns = [scale[:, c : c + 1] for scale in scales]
        masses.append(
            sum(col * (t[:, 2 + 2 * c : 3 + 2 * c] + t[:, 3 + 2 * c : 4 + 2 * c]) for col, t in zip(columns, tiles))
        )
        inputs.append(sum(col * load(c * width, width) for col, load in zip(columns, blocks)))
        grads.append(sum(load((2 + c) * width, width) for load in blocks))
    return inputs, grads, peaks, masses


def loader(ref, index):
    return lambda at, size: ref[index, :, pl.ds(at, size)].astype(F32)


def stat_tile(peaks, masses):
    return packed([peaks[0], peaks[1], *pieces(masses[0], 2), *pieces(masses[1], 2)])


def merge_cores(keep_ref, recv_ref, out_ref):
    width = (keep_ref.shape[2] - LANES) // 4
    for q in range(keep_ref.shape[0]):
        inputs, grads, peaks, masses = merged([loader(keep_ref, q), loader(recv_ref, q)], width)
        for k, value in enumerate(inputs + grads):
            out_ref[q, :, pl.ds(k * width, width)] = value.astype(BF16)
        out_ref[q, :, pl.ds(4 * width, LANES)] = stat_tile(peaks, masses).astype(BF16)


def merge_column(in_ref, out_ref):
    width = (in_ref.shape[2] - LANES) // 4
    blocks = [loader(in_ref, k) for k in range(in_ref.shape[0])]
    inputs, grads, peaks, masses = merged(blocks, width)
    for k, value in enumerate(inputs + grads):
        for q in range(out_ref.shape[0]):
            out_ref[q, :, pl.ds(k * width, width)] = value.astype(BF16)
    for q in range(out_ref.shape[0]):
        out_ref[q, :, pl.ds(4 * width, LANES)] = stat_tile(peaks, masses).astype(BF16)


GELU_A = 0.7978845608028654
GELU_B = 0.044715


def experts(in_ref, w_in_ref, w_out_ref, out_ref, rows_ref, grads_ref, hidden_ref, pre_grad_ref, slot_in_ref, stats_ref):
    width = w_in_ref.shape[1]
    count = w_in_ref.shape[0]
    blocks = [loader(in_ref, k) for k in range(in_ref.shape[0])]
    inputs, grads, peaks, masses = merged(blocks, width)
    slot_in = jnp.concatenate([value / mass for value, mass in zip(inputs, masses)], axis=0)
    slot_in_ref[...] = slot_in
    stats_ref[...] = packed([*peaks, *pieces(masses[0], 3), *pieces(masses[1], 3)])
    x = slot_in.astype(BF16)
    g = jnp.concatenate(grads, axis=0).astype(BF16)
    rows_ref[...] = x
    grads_ref[...] = g
    total = x.shape[0]
    hid = w_in_ref.shape[2]
    owner = lambda shape: lax.rem(lax.broadcasted_iota(jnp.int32, shape, 0), GROUP) // (GROUP // count)
    who = owner((total, hid))
    pre = jnp.zeros((total, hid), F32)
    hidden_grad = jnp.zeros((total, hid), F32)
    for e in range(count):
        pre = jnp.where(who == e, dot_nn(x, w_in_ref[e]), pre)
        hidden_grad = jnp.where(who == e, dot_nt(g, w_out_ref[e]), hidden_grad)
    inner = jnp.tanh(GELU_A * (pre + GELU_B * pre * pre * pre))
    hidden = 0.5 * pre * (1.0 + inner)
    slope = 0.5 * (1.0 + inner) + 0.5 * pre * (1.0 - inner * inner) * GELU_A * (1.0 + 3.0 * GELU_B * pre * pre)
    pre_grad = hidden_grad * slope
    hidden_ref[...] = hidden.astype(BF16)
    pre_grad_ref[...] = pre_grad.astype(BF16)
    out_part = jnp.zeros((total, width), F32)
    in_part = jnp.zeros((total, width), F32)
    for e in range(count):
        out_part += dot_nn(jnp.where(who == e, hidden, 0.0).astype(BF16), w_out_ref[e])
        in_part += dot_nt(jnp.where(who == e, pre_grad, 0.0).astype(BF16), w_in_ref[e])
    both = jnp.concatenate([out_part, in_part], axis=0).astype(BF16)
    for q in range(out_ref.shape[0]):
        out_ref[q] = both


def run_experts(sums, w_in, w_out):
    count, width, hid = w_in.shape
    peers = sums.shape[0]
    rows = 2 * GROUP
    return pl.pallas_call(
        experts,
        out_shape=[
            jax.ShapeDtypeStruct((peers, 2 * rows, width), BF16),
            jax.ShapeDtypeStruct((rows, width), BF16),
            jax.ShapeDtypeStruct((rows, width), BF16),
            jax.ShapeDtypeStruct((rows, hid), BF16),
            jax.ShapeDtypeStruct((rows, hid), BF16),
            jax.ShapeDtypeStruct((rows, width), F32),
            jax.ShapeDtypeStruct((GROUP, LANES), F32),
        ],
        compiler_params=params(16),
        name="experts",
    )(sums, w_in, w_out)


def weight_grads(rows_ref, grads_ref, hidden_ref, pre_grad_ref, w_in_grad_ref, w_out_grad_ref):
    e = pl.program_id(0)
    total, hid = hidden_ref.shape
    count = pl.num_programs(0)
    who = lax.rem(lax.broadcasted_iota(jnp.int32, (total, hid), 0), GROUP) // (GROUP // 2)
    mask = who == e
    hidden = jnp.where(mask, hidden_ref[...].astype(F32), 0.0).astype(BF16)
    pre_grad = jnp.where(mask, pre_grad_ref[...].astype(F32), 0.0).astype(BF16)
    w_out_grad_ref[0] = dot_tn(hidden, grads_ref[...]).astype(BF16)
    w_in_grad_ref[0] = dot_tn(rows_ref[...], pre_grad).astype(BF16)


def run_weight_grads(rows, grads, hidden, pre_grad, count):
    total, width = rows.shape
    hid = hidden.shape[1]
    whole = lambda *shape: pl.BlockSpec(shape, lambda e: (0,) * len(shape))
    return pl.pallas_call(
        weight_grads,
        grid=(count,),
        in_specs=[whole(total, width), whole(total, width), whole(total, hid), whole(total, hid)],
        out_specs=[
            pl.BlockSpec((1, width, hid), lambda e: (e, 0, 0)),
            pl.BlockSpec((1, hid, width), lambda e: (e, 0, 0)),
        ],
        out_shape=[
            jax.ShapeDtypeStruct((count, width, hid), BF16),
            jax.ShapeDtypeStruct((count, hid, width), BF16),
        ],
        compiler_params=params(16, 1),
        cost_estimate=pl.CostEstimate(
            flops=4 * count * total * width * hid, transcendentals=0, bytes_accessed=4 * count * width * hid
        ),
        name="weight_grads",
    )(rows, grads, hidden, pre_grad)


def slot_results(in_ref, slot_in_ref, stats_ref, out_ref):
    width = in_ref.shape[2]
    total = sum(in_ref[k].astype(F32) for k in range(in_ref.shape[0])).astype(BF16)
    back = total[2 * GROUP :].astype(F32)
    inner = jnp.sum(back * slot_in_ref[...], axis=1, keepdims=True)
    tile = stats_ref[...]
    lane = lax.broadcasted_iota(jnp.int32, tile.shape, 1)
    for c in range(2):
        for k, column in enumerate(pieces(inner[c * GROUP : (c + 1) * GROUP], 3)):
            tile = jnp.where(lane == 8 + 3 * c + k, column, tile)
    for q in range(out_ref.shape[0]):
        for k in range(4):
            out_ref[q, :, pl.ds(k * width, width)] = total[k * GROUP : (k + 1) * GROUP]
        out_ref[q, :, pl.ds(4 * width, LANES)] = tile.astype(BF16)


def turn(in_ref, out_ref):
    rows = in_ref.shape[1]
    for c in range(in_ref.shape[0]):
        out_ref[:, pl.ds(c * rows, rows)] = in_ref[c].T


def half_products(tok_t_ref, grad_t_ref, slots_ref, outs_ref, backs_ref, stats_ref, dispatch_grad_ref, mixing_grad_ref):
    clips, rows = outs_ref.shape[0], dispatch_grad_ref.shape[2]
    width = outs_ref.shape[2]
    for q in range(slots_ref.shape[0]):
        at = pl.ds(q * GROUP, GROUP)
        for c in range(clips):
            outs_ref[c, at, :] = slots_ref[q, :, pl.ds(c * width, width)]
            backs_ref[c, at, :] = slots_ref[q, :, pl.ds((2 + c) * width, width)]
        stats_ref[at, :] = slots_ref[q, :, pl.ds(4 * width, LANES)].astype(F32)
    for c in range(clips):
        at = pl.ds(c * rows, rows)
        dispatch_grad_ref[c] = dot_nn(backs_ref[c], tok_t_ref[:, at])
        mixing_grad_ref[c] = dot_nn(outs_ref[c], grad_t_ref[:, at])


def run_half_products(tok_t, grad_t, slots, clips):
    half, width = slots.shape[0] * GROUP, tok_t.shape[0]
    rows = tok_t.shape[1] // clips
    shapes = [
        ((clips, half, width), BF16),
        ((clips, half, width), BF16),
        ((half, LANES), F32),
        ((clips, half, rows), F32),
        ((clips, half, rows), F32),
    ]
    return pl.pallas_call(
        half_products,
        in_specs=[VMEM] * 3,
        out_specs=[VMEM] * len(shapes),
        out_shape=[jax.ShapeDtypeStruct(*shape) for shape in shapes],
        compiler_params=params(16),
        name="half_products",
    )(tok_t, grad_t, slots)


def second_pass(
    tok_ref, tok_t_ref, grad_t_ref, terms_ref, mixing_ref, local_ref,
    own_stats_ref, own_dispatch_ref, own_mixing_ref, slots_ref,
    outs_ref, backs_ref, weights_ref, part_ref, stats_ref, other_dispatch_ref, other_mixing_ref, ordered,
):
    core = lax.axis_index(CORE)
    clips, rows, width = tok_ref.shape
    slots = terms_ref.shape[1]
    half = slots // 2
    half_products(
        tok_t_ref, grad_t_ref, slots_ref, outs_ref, backs_ref, stats_ref, other_dispatch_ref, other_mixing_ref
    )
    tile = jnp.concatenate([own_stats_ref[...], stats_ref[...]], axis=0)
    local = local_ref[...]
    column = lambda k: tile[:, k : k + 1]
    total = jnp.zeros((slots, width), F32)
    for c in range(clips):
        mass = column(2 + 3 * c) + column(3 + 3 * c) + column(4 + 3 * c)
        inner = column(8 + 3 * c) + column(9 + 3 * c) + column(10 + 3 * c)
        scale = jnp.exp(local[:, c : c + 1] - column(c)) / mass
        dispatch = terms_ref[c] * scale
        weights_ref[c, pl.ds(0, slots), :] = dispatch.astype(BF16)
        mixing = mixing_ref[c]
        dispatch_grad = jnp.concatenate([own_dispatch_ref[c], other_dispatch_ref[c]], axis=0)
        mixing_grad = jnp.concatenate([own_mixing_ref[c], other_mixing_ref[c]], axis=0)
        logit_grad = dispatch * (dispatch_grad - inner) + mixing * (
            mixing_grad - jnp.sum(mixing * mixing_grad, axis=0, keepdims=True)
        )
        logit_b = logit_grad.astype(BF16)
        weights_ref[c, pl.ds(slots, slots), :] = logit_b
        total = total + dot_nn(logit_b, tok_ref[c])
    for k in range(slots // GROUP):
        place = k % (half // GROUP)
        side = core if k < half // GROUP else 1 - core
        at = pl.ds(pl.multiple_of((2 * place + side) * GROUP, GROUP), GROUP)
        ordered[at, :] = total[k * GROUP : (k + 1) * GROUP]
    part_ref[...] = ordered[...].T.astype(BF16)


def run_second_pass(tok, tok_t, grad_t, terms, mixing, local, own, other):
    clips, rows, width = tok.shape
    slots = terms.shape[1]
    shapes = [(clips, slots // 2, width), (clips, slots // 2, width), (clips, 2 * slots, rows), (width, slots)]
    return pl.pallas_call(
        second_pass,
        in_specs=[VMEM] * 10,
        out_specs=[VMEM] * len(shapes),
        out_shape=[jax.ShapeDtypeStruct(shape, BF16) for shape in shapes],
        scratch_shapes=[
            pltpu.VMEM((slots // 2, LANES), F32),
            pltpu.VMEM((clips, slots // 2, rows), F32),
            pltpu.VMEM((clips, slots // 2, rows), F32),
            pltpu.VMEM((slots, width), F32),
        ],
        compiler_params=params(24),
        name="second_pass",
    )(tok, tok_t, grad_t, terms, mixing, local, *own, other)


def token_outputs(
    mix_ref, weights_ref, own_outs_ref, other_outs_ref, own_backs_ref, other_backs_ref, router_t_ref,
    mixed_ref, grad_tokens_ref,
):
    outs = jnp.concatenate([own_outs_ref[0], other_outs_ref[0]], axis=0)
    backs = jnp.concatenate([own_backs_ref[0], other_backs_ref[0], router_t_ref[...]], axis=0)
    mixed_ref[0] = dot_tn(mix_ref[0], outs).astype(BF16)
    grad_tokens_ref[0] = dot_tn(weights_ref[0], backs).astype(BF16)


def run_token_outputs(mix, weights, own_outs, other_outs, own_backs, other_backs, router_t):
    clips, slots, rows = mix.shape
    width = own_outs.shape[2]
    block = 384
    out = pl.BlockSpec((1, block, width), lambda c, t: (c, t, 0))
    part = pl.BlockSpec((1, slots // 2, width), lambda c, t: (c, 0, 0))
    return pl.pallas_call(
        token_outputs,
        grid=(clips, rows // block),
        in_specs=[
            pl.BlockSpec((1, slots, block), lambda c, t: (c, 0, t)),
            pl.BlockSpec((1, 2 * slots, block), lambda c, t: (c, 0, t)),
            part,
            part,
            part,
            part,
            pl.BlockSpec((slots, width), lambda c, t: (0, 0)),
        ],
        out_specs=[out, out],
        out_shape=[jax.ShapeDtypeStruct((clips, rows, width), BF16)] * 2,
        compiler_params=params(16, 2),
        cost_estimate=pl.CostEstimate(
            flops=6 * clips * rows * slots * width, transcendentals=0, bytes_accessed=6 * clips * rows * width
        ),
        name="token_outputs",
    )(mix, weights, own_outs, other_outs, own_backs, other_backs, router_t)


def add_up(in_ref, out_ref):
    rows, total = out_ref.shape[0], in_ref.shape[0]
    row = lax.broadcasted_iota(jnp.int32, (rows, total), 0)
    at = lax.broadcasted_iota(jnp.int32, (rows, total), 1)
    pick = jnp.where(lax.rem(at, rows) == row, 1.0, 0.0).astype(BF16)
    out_ref[...] = dot_nn(pick, in_ref[...])


def exchanged(array, axes):
    return lax.all_to_all(array, axes, split_axis=0, concat_axis=0, tiled=True)


def swapped(array):
    return lax.ppermute(array, CORE, [(0, 1), (1, 0)])


def on_device(tokens, router, w_in, w_out, grad_out):
    peers = lax.axis_size(SEQ)
    width = tokens.shape[2]
    row = 4 * width + LANES
    chips = lax.axis_size(CHIPS_EXP)
    tok, tok_t, grad, router_t, terms, mixing, mix, local, keep, send = run_first_pass(tokens, router, grad_out)
    recv = swapped(send)
    small = params(16)
    grad_t = pl.pallas_call(
        turn,
        in_specs=[VMEM],
        out_specs=VMEM,
        out_shape=jax.ShapeDtypeStruct(tok_t.shape, BF16),
        compiler_params=small,
        name="turn",
    )(grad)
    recv, grad_t = lax.optimization_barrier((recv, grad_t))
    halves = pl.pallas_call(
        merge_cores, out_shape=jax.ShapeDtypeStruct((chips, GROUP, row), BF16), compiler_params=small, name="merge_cores"
    )(keep, recv)
    column = pl.pallas_call(
        merge_column, out_shape=jax.ShapeDtypeStruct((peers, GROUP, row), BF16), compiler_params=small, name="merge_column"
    )(exchanged(halves, CHIPS_EXP))
    parts, rows, grads, hidden, pre_grad, slot_in, stats = run_experts(exchanged(column, SEQ), w_in, w_out)
    arrived = exchanged(parts, SEQ)
    grad_w_in, grad_w_out = run_weight_grads(rows, grads, hidden, pre_grad, w_in.shape[0])
    results = pl.pallas_call(
        slot_results, out_shape=jax.ShapeDtypeStruct((chips, GROUP, row), BF16), compiler_params=small, name="slot_results"
    )(arrived, slot_in, stats)
    mine = exchanged(results, CHIPS_EXP)
    other = swapped(mine)
    own_outs, own_backs, *own = run_half_products(tok_t, grad_t, mine, tokens.shape[0])
    other, *own = lax.optimization_barrier((other, *own))
    other_outs, other_backs, weights, part = run_second_pass(tok, tok_t, grad_t, terms, mixing, local, own, other)
    devices = lax.axis_size(SEQ_EXP)
    arrived = exchanged(part.reshape(devices, width // devices, part.shape[1]), SEQ_EXP)
    mixed, grad_tokens = run_token_outputs(mix, weights, own_outs, other_outs, own_backs, other_backs, router_t)
    grad_router = pl.pallas_call(
        add_up, out_shape=jax.ShapeDtypeStruct(arrived.shape[1:], F32), compiler_params=small, name="add_up"
    )(arrived.reshape(width, part.shape[1]))
    return (mixed, grad_tokens, grad_router, grad_w_in, grad_w_out)


def solution(mesh):
    finer = Mesh(mesh.devices.reshape(2, 4, 2, 4, 2), SEQ_EXP)
    return jax.shard_map(
        on_device,
        mesh=finer,
        in_specs=(
            P(None, SEQ_EXP, None),
            P(),
            P(EXP, None, SEQ),
            P(EXP, SEQ, None),
            P(None, SEQ_EXP, None),
        ),
        out_specs=(
            P(None, SEQ_EXP, None),
            P(None, SEQ_EXP, None),
            P(SEQ_EXP, None),
            P(EXP, None, SEQ),
            P(EXP, SEQ, None),
        ),
        check_vma=False,
    )
```

```python
import functools

import jax
import jax.numpy as jnp
from jax import lax
from jax.experimental import pallas as pl
from jax.experimental.pallas import tpu as pltpu
from jax.sharding import Mesh
from jax.sharding import PartitionSpec as P

SEQ = ("seq_0", "seq_1")
EXP = ("exp_0", "exp_1", "exp_2")
CHIPS_EXP = ("exp_0", "exp_1")
CORE = "exp_2"
SEQ_EXP = SEQ + EXP

F32 = jnp.float32
BF16 = jnp.bfloat16
LANES = 128
GROUP = 8


def dot_nt(a, b):
    return lax.dot_general(a, b, (((1,), (1,)), ((), ())), preferred_element_type=F32)


def dot_nn(a, b):
    return lax.dot_general(a, b, (((1,), (0,)), ((), ())), preferred_element_type=F32)


def dot_tn(a, b):
    return lax.dot_general(a, b, (((0,), (0,)), ((), ())), preferred_element_type=F32)


def params(mib, grid_dims=0):
    kinds = ("arbitrary",) * grid_dims if grid_dims else None
    return pltpu.CompilerParams(vmem_limit_bytes=mib << 20, dimension_semantics=kinds)


def pieces(value, count):
    found = []
    for _ in range(count):
        part = value.astype(BF16).astype(F32)
        found.append(part)
        value = value - part
    return found


def packed(columns):
    rows = columns[0].shape[0]
    lane = lax.broadcasted_iota(jnp.int32, (rows, LANES), 1)
    tile = jnp.zeros((rows, LANES), F32)
    for k, column in enumerate(columns):
        tile = jnp.where(lane == k, column, tile)
    return tile


def mixing_of(logits_t):
    peak = jnp.max(logits_t, axis=0, keepdims=True)
    terms = jnp.exp(logits_t - peak)
    return terms * (1.0 / jnp.sum(terms, axis=0, keepdims=True))


def first_pass(
    tok_hbm, router_hbm, grad_hbm,
    tok_ref, tok_t_ref, grad_ref, router_t_ref, terms_ref, mixing_ref, mix_ref, stats_ref, keep_ref, send_ref,
    router_buf, router_f, sems,
):
    core = lax.axis_index(CORE)
    clips, rows, width = tok_ref.shape
    slots = router_t_ref.shape[0]
    half = slots // 2
    copies = [pltpu.make_async_copy(router_hbm, router_buf, sems.at[0])]
    for c in range(clips):
        copies.append(pltpu.make_async_copy(tok_hbm.at[c], tok_ref.at[c], sems.at[1 + c]))
    for c in range(clips):
        copies.append(pltpu.make_async_copy(grad_hbm.at[c], grad_ref.at[c], sems.at[1 + clips + c]))
    for copy in copies:
        copy.start()
    copies[0].wait()
    router_f[...] = router_buf[...].T.astype(F32)
    for k in range(slots // GROUP):
        place = k % (half // GROUP)
        side = core if k < half // GROUP else 1 - core
        at = pl.ds(pl.multiple_of((2 * place + side) * GROUP, GROUP), GROUP)
        router_t_ref[pl.ds(k * GROUP, GROUP), :] = router_f[at, :].astype(BF16)
    columns = [None] * 12
    for c in range(clips):
        copies[1 + c].wait()
        tok_t_ref[:, pl.ds(c * rows, rows)] = tok_ref[c].T
    both = dot_nn(router_t_ref[...], tok_t_ref[...])
    for c in range(clips):
        logits_t = both[:, c * rows : (c + 1) * rows]
        peak = jnp.max(logits_t, axis=1, keepdims=True)
        terms = jnp.exp(logits_t - peak)
        terms_ref[c] = terms
        mass = jnp.sum(terms, axis=1, keepdims=True)
        columns[3 * c : 3 * c + 3] = pieces(peak, 3)
        columns[6 + 3 * c : 9 + 3 * c] = pieces(mass, 3)
        sums = dot_nn(terms.astype(BF16), tok_ref[c]).astype(BF16)
        mixing = mixing_of(logits_t)
        mixing_ref[c] = mixing
        mix_ref[c] = mixing.astype(BF16)
        for q in range(keep_ref.shape[0]):
            at = pl.ds(c * width, width)
            keep_ref[q, :, at] = sums[q * GROUP : (q + 1) * GROUP]
            send_ref[q, :, at] = sums[half + q * GROUP : half + (q + 1) * GROUP]
    for c in range(clips):
        copies[1 + clips + c].wait()
    stats = packed(columns)
    stats_ref[...] = stats
    stats = stats.astype(BF16)
    for q in range(keep_ref.shape[0]):
        at = pl.ds(4 * width, LANES)
        keep_ref[q, :, at] = stats[q * GROUP : (q + 1) * GROUP]
        send_ref[q, :, at] = stats[half + q * GROUP : half + (q + 1) * GROUP]
    for c in range(clips):
        sums = dot_nn(mix_ref[c], grad_ref[c]).astype(BF16)
        for q in range(keep_ref.shape[0]):
            at = pl.ds((2 + c) * width, width)
            keep_ref[q, :, at] = sums[q * GROUP : (q + 1) * GROUP]
            send_ref[q, :, at] = sums[half + q * GROUP : half + (q + 1) * GROUP]


VMEM = pl.BlockSpec(memory_space=pltpu.VMEM)
HBM = pl.BlockSpec(memory_space=pltpu.HBM)


def run_first_pass(tokens, router, grad_out):
    clips, rows, width = tokens.shape
    slots = router.shape[1]
    row = 4 * width + LANES
    groups = slots // GROUP // 2
    shapes = [
        (tokens.shape, BF16),
        ((width, clips * rows), BF16),
        (grad_out.shape, BF16),
        ((slots, width), BF16),
        ((clips, slots, rows), F32),
        ((clips, slots, rows), F32),
        ((clips, slots, rows), BF16),
        ((slots, LANES), F32),
        ((groups, GROUP, row), BF16),
        ((groups, GROUP, row), BF16),
    ]
    return pl.pallas_call(
        first_pass,
        in_specs=[HBM] * 3,
        out_specs=[VMEM] * len(shapes),
        out_shape=[jax.ShapeDtypeStruct(*shape) for shape in shapes],
        scratch_shapes=[
            pltpu.VMEM(router.shape, BF16),
            pltpu.VMEM((slots, width), F32),
            pltpu.SemaphoreType.DMA((1 + 2 * clips,)),
        ],
        compiler_params=params(28),
        name="first_pass",
    )(*(pltpu.with_memory_space_constraint(a, pltpu.HBM) for a in (tokens, router, grad_out)))


def whole_of(tile, at):
    return tile[:, at : at + 1] + tile[:, at + 1 : at + 2] + tile[:, at + 2 : at + 3]


def merged(blocks, width):
    tiles = [load(4 * width, LANES) for load in blocks]
    inputs, grads, peaks, masses = [], [], [], []
    for c in range(2):
        tops = [whole_of(tile, 3 * c) for tile in tiles]
        peaks.append(functools.reduce(jnp.maximum, tops))
        columns = [jnp.exp(top - peaks[c]) for top in tops]
        masses.append(sum(col * whole_of(tile, 6 + 3 * c) for col, tile in zip(columns, tiles)))
        inputs.append(sum(col * load(c * width, width) for col, load in zip(columns, blocks)))
        grads.append(sum(load((2 + c) * width, width) for load in blocks))
    return inputs, grads, peaks, masses


def loader(ref, index):
    return lambda at, size: ref[index, :, pl.ds(at, size)].astype(F32)


def stat_tile(peaks, masses):
    return packed([piece for value in (*peaks, *masses) for piece in pieces(value, 3)])


def merge_cores(keep_ref, recv_ref, out_ref):
    width = (keep_ref.shape[2] - LANES) // 4
    for q in range(keep_ref.shape[0]):
        inputs, grads, peaks, masses = merged([loader(keep_ref, q), loader(recv_ref, q)], width)
        for k, value in enumerate(inputs + grads):
            out_ref[q, :, pl.ds(k * width, width)] = value.astype(BF16)
        out_ref[q, :, pl.ds(4 * width, LANES)] = stat_tile(peaks, masses).astype(BF16)


def merge_column(in_ref, out_ref):
    width = (in_ref.shape[2] - LANES) // 4
    blocks = [loader(in_ref, k) for k in range(in_ref.shape[0])]
    inputs, grads, peaks, masses = merged(blocks, width)
    for k, value in enumerate(inputs + grads):
        for q in range(out_ref.shape[0]):
            out_ref[q, :, pl.ds(k * width, width)] = value.astype(BF16)
    for q in range(out_ref.shape[0]):
        out_ref[q, :, pl.ds(4 * width, LANES)] = stat_tile(peaks, masses).astype(BF16)


GELU_A = 0.7978845608028654
GELU_B = 0.044715


def experts(in_ref, w_in_ref, w_out_ref, out_ref, rows_ref, grads_ref, hidden_ref, pre_grad_ref, slot_in_ref, stats_ref):
    width = w_in_ref.shape[1]
    count = w_in_ref.shape[0]
    blocks = [loader(in_ref, k) for k in range(in_ref.shape[0])]
    inputs, grads, peaks, masses = merged(blocks, width)
    slot_in = jnp.concatenate([value / mass for value, mass in zip(inputs, masses)], axis=0)
    slot_in_ref[...] = slot_in
    stats_ref[...] = stat_tile(peaks, masses)
    x = slot_in.astype(BF16)
    g = jnp.concatenate(grads, axis=0).astype(BF16)
    rows_ref[...] = x
    grads_ref[...] = g
    total = x.shape[0]
    hid = w_in_ref.shape[2]
    owner = lambda shape: lax.rem(lax.broadcasted_iota(jnp.int32, shape, 0), GROUP) // (GROUP // count)
    who = owner((total, hid))
    pre = jnp.zeros((total, hid), F32)
    hidden_grad = jnp.zeros((total, hid), F32)
    for e in range(count):
        pre = jnp.where(who == e, dot_nn(x, w_in_ref[e]), pre)
        hidden_grad = jnp.where(who == e, dot_nt(g, w_out_ref[e]), hidden_grad)
    inner = jnp.tanh(GELU_A * (pre + GELU_B * pre * pre * pre))
    hidden = 0.5 * pre * (1.0 + inner)
    slope = 0.5 * (1.0 + inner) + 0.5 * pre * (1.0 - inner * inner) * GELU_A * (1.0 + 3.0 * GELU_B * pre * pre)
    pre_grad = hidden_grad * slope
    hidden_ref[...] = hidden.astype(BF16)
    pre_grad_ref[...] = pre_grad.astype(BF16)
    out_part = jnp.zeros((total, width), F32)
    in_part = jnp.zeros((total, width), F32)
    for e in range(count):
        out_part += dot_nn(jnp.where(who == e, hidden, 0.0).astype(BF16), w_out_ref[e])
        in_part += dot_nt(jnp.where(who == e, pre_grad, 0.0).astype(BF16), w_in_ref[e])
    both = jnp.concatenate([out_part, in_part], axis=0).astype(BF16)
    for q in range(out_ref.shape[0]):
        out_ref[q] = both


def run_experts(sums, w_in, w_out):
    count, width, hid = w_in.shape
    peers = sums.shape[0]
    rows = 2 * GROUP
    return pl.pallas_call(
        experts,
        out_shape=[
            jax.ShapeDtypeStruct((peers, 2 * rows, width), BF16),
            jax.ShapeDtypeStruct((rows, width), BF16),
            jax.ShapeDtypeStruct((rows, width), BF16),
            jax.ShapeDtypeStruct((rows, hid), BF16),
            jax.ShapeDtypeStruct((rows, hid), BF16),
            jax.ShapeDtypeStruct((rows, width), F32),
            jax.ShapeDtypeStruct((GROUP, LANES), F32),
        ],
        compiler_params=params(16),
        name="experts",
    )(sums, w_in, w_out)


def weight_grads(rows_ref, grads_ref, hidden_ref, pre_grad_ref, w_in_grad_ref, w_out_grad_ref):
    e = pl.program_id(0)
    total, hid = hidden_ref.shape
    count = pl.num_programs(0)
    who = lax.rem(lax.broadcasted_iota(jnp.int32, (total, hid), 0), GROUP) // (GROUP // 2)
    mask = who == e
    hidden = jnp.where(mask, hidden_ref[...].astype(F32), 0.0).astype(BF16)
    pre_grad = jnp.where(mask, pre_grad_ref[...].astype(F32), 0.0).astype(BF16)
    w_out_grad_ref[0] = dot_tn(hidden, grads_ref[...]).astype(BF16)
    w_in_grad_ref[0] = dot_tn(rows_ref[...], pre_grad).astype(BF16)


def run_weight_grads(rows, grads, hidden, pre_grad, count):
    total, width = rows.shape
    hid = hidden.shape[1]
    whole = lambda *shape: pl.BlockSpec(shape, lambda e: (0,) * len(shape))
    return pl.pallas_call(
        weight_grads,
        grid=(count,),
        in_specs=[whole(total, width), whole(total, width), whole(total, hid), whole(total, hid)],
        out_specs=[
            pl.BlockSpec((1, width, hid), lambda e: (e, 0, 0)),
            pl.BlockSpec((1, hid, width), lambda e: (e, 0, 0)),
        ],
        out_shape=[
            jax.ShapeDtypeStruct((count, width, hid), BF16),
            jax.ShapeDtypeStruct((count, hid, width), BF16),
        ],
        compiler_params=params(16, 1),
        cost_estimate=pl.CostEstimate(
            flops=4 * count * total * width * hid, transcendentals=0, bytes_accessed=4 * count * width * hid
        ),
        name="weight_grads",
    )(rows, grads, hidden, pre_grad)


def slot_results(in_ref, slot_in_ref, stats_ref, out_ref):
    width = in_ref.shape[2]
    total = sum(in_ref[k].astype(F32) for k in range(in_ref.shape[0])).astype(BF16)
    back = total[2 * GROUP :].astype(F32)
    inner = jnp.sum(back * slot_in_ref[...], axis=1, keepdims=True)
    tile = stats_ref[...]
    lane = lax.broadcasted_iota(jnp.int32, tile.shape, 1)
    for c in range(2):
        for k, column in enumerate(pieces(inner[c * GROUP : (c + 1) * GROUP], 3)):
            tile = jnp.where(lane == 12 + 3 * c + k, column, tile)
    for q in range(out_ref.shape[0]):
        for k in range(4):
            out_ref[q, :, pl.ds(k * width, width)] = total[k * GROUP : (k + 1) * GROUP]
        out_ref[q, :, pl.ds(4 * width, LANES)] = tile.astype(BF16)


def turn(in_ref, out_ref):
    rows = in_ref.shape[1]
    for c in range(in_ref.shape[0]):
        out_ref[:, pl.ds(c * rows, rows)] = in_ref[c].T


def half_products(tok_t_ref, grad_t_ref, slots_ref, outs_ref, backs_ref, stats_ref, dispatch_grad_ref, mixing_grad_ref):
    clips, rows = outs_ref.shape[0], dispatch_grad_ref.shape[2]
    width = outs_ref.shape[2]
    for q in range(slots_ref.shape[0]):
        at = pl.ds(q * GROUP, GROUP)
        for c in range(clips):
            outs_ref[c, at, :] = slots_ref[q, :, pl.ds(c * width, width)]
            backs_ref[c, at, :] = slots_ref[q, :, pl.ds((2 + c) * width, width)]
        stats_ref[at, :] = slots_ref[q, :, pl.ds(4 * width, LANES)].astype(F32)
    for c in range(clips):
        at = pl.ds(c * rows, rows)
        dispatch_grad_ref[c] = dot_nn(backs_ref[c], tok_t_ref[:, at])
        mixing_grad_ref[c] = dot_nn(outs_ref[c], grad_t_ref[:, at])


def run_half_products(tok_t, grad_t, slots, clips):
    half, width = slots.shape[0] * GROUP, tok_t.shape[0]
    rows = tok_t.shape[1] // clips
    shapes = [
        ((clips, half, width), BF16),
        ((clips, half, width), BF16),
        ((half, LANES), F32),
        ((clips, half, rows), F32),
        ((clips, half, rows), F32),
    ]
    return pl.pallas_call(
        half_products,
        in_specs=[VMEM] * 3,
        out_specs=[VMEM] * len(shapes),
        out_shape=[jax.ShapeDtypeStruct(*shape) for shape in shapes],
        compiler_params=params(16),
        name="half_products",
    )(tok_t, grad_t, slots)


def second_pass(
    tok_ref, tok_t_ref, grad_t_ref, terms_ref, mixing_ref, local_ref,
    own_stats_ref, own_dispatch_ref, own_mixing_ref, slots_ref,
    outs_ref, backs_ref, weights_ref, part_ref, stats_ref, other_dispatch_ref, other_mixing_ref, ordered,
):
    core = lax.axis_index(CORE)
    clips, rows, width = tok_ref.shape
    slots = terms_ref.shape[1]
    half = slots // 2
    half_products(
        tok_t_ref, grad_t_ref, slots_ref, outs_ref, backs_ref, stats_ref, other_dispatch_ref, other_mixing_ref
    )
    tile = jnp.concatenate([own_stats_ref[...], stats_ref[...]], axis=0)
    local = local_ref[...]
    total = jnp.zeros((slots, width), F32)
    for c in range(clips):
        mass, inner = whole_of(tile, 6 + 3 * c), whole_of(tile, 12 + 3 * c)
        scale = jnp.exp(whole_of(local, 3 * c) - whole_of(tile, 3 * c)) / mass
        dispatch = terms_ref[c] * scale
        weights_ref[c, pl.ds(0, slots), :] = dispatch.astype(BF16)
        mixing = mixing_ref[c]
        dispatch_grad = jnp.concatenate([own_dispatch_ref[c], other_dispatch_ref[c]], axis=0)
        mixing_grad = jnp.concatenate([own_mixing_ref[c], other_mixing_ref[c]], axis=0)
        logit_grad = dispatch * (dispatch_grad - inner) + mixing * (
            mixing_grad - jnp.sum(mixing * mixing_grad, axis=0, keepdims=True)
        )
        logit_b = logit_grad.astype(BF16)
        weights_ref[c, pl.ds(slots, slots), :] = logit_b
        total = total + dot_nn(logit_b, tok_ref[c])
    for k in range(slots // GROUP):
        place = k % (half // GROUP)
        side = core if k < half // GROUP else 1 - core
        at = pl.ds(pl.multiple_of((2 * place + side) * GROUP, GROUP), GROUP)
        ordered[at, :] = total[k * GROUP : (k + 1) * GROUP]
    part_ref[...] = ordered[...].T.astype(BF16)


def run_second_pass(tok, tok_t, grad_t, terms, mixing, local, own, other):
    clips, rows, width = tok.shape
    slots = terms.shape[1]
    shapes = [(clips, slots // 2, width), (clips, slots // 2, width), (clips, 2 * slots, rows), (width, slots)]
    return pl.pallas_call(
        second_pass,
        in_specs=[VMEM] * 10,
        out_specs=[VMEM] * len(shapes),
        out_shape=[jax.ShapeDtypeStruct(shape, BF16) for shape in shapes],
        scratch_shapes=[
            pltpu.VMEM((slots // 2, LANES), F32),
            pltpu.VMEM((clips, slots // 2, rows), F32),
            pltpu.VMEM((clips, slots // 2, rows), F32),
            pltpu.VMEM((slots, width), F32),
        ],
        compiler_params=params(24),
        name="second_pass",
    )(tok, tok_t, grad_t, terms, mixing, local, *own, other)


def token_outputs(
    mix_ref, weights_ref, own_outs_ref, other_outs_ref, own_backs_ref, other_backs_ref, router_t_ref,
    mixed_ref, grad_tokens_ref,
):
    outs = jnp.concatenate([own_outs_ref[0], other_outs_ref[0]], axis=0)
    backs = jnp.concatenate([own_backs_ref[0], other_backs_ref[0], router_t_ref[...]], axis=0)
    mixed_ref[0] = dot_tn(mix_ref[0], outs).astype(BF16)
    grad_tokens_ref[0] = dot_tn(weights_ref[0], backs).astype(BF16)


def run_token_outputs(mix, weights, own_outs, other_outs, own_backs, other_backs, router_t):
    clips, slots, rows = mix.shape
    width = own_outs.shape[2]
    block = 384
    out = pl.BlockSpec((1, block, width), lambda c, t: (c, t, 0))
    part = pl.BlockSpec((1, slots // 2, width), lambda c, t: (c, 0, 0))
    return pl.pallas_call(
        token_outputs,
        grid=(clips, rows // block),
        in_specs=[
            pl.BlockSpec((1, slots, block), lambda c, t: (c, 0, t)),
            pl.BlockSpec((1, 2 * slots, block), lambda c, t: (c, 0, t)),
            part,
            part,
            part,
            part,
            pl.BlockSpec((slots, width), lambda c, t: (0, 0)),
        ],
        out_specs=[out, out],
        out_shape=[jax.ShapeDtypeStruct((clips, rows, width), BF16)] * 2,
        compiler_params=params(16, 2),
        cost_estimate=pl.CostEstimate(
            flops=6 * clips * rows * slots * width, transcendentals=0, bytes_accessed=6 * clips * rows * width
        ),
        name="token_outputs",
    )(mix, weights, own_outs, other_outs, own_backs, other_backs, router_t)


def add_up(in_ref, out_ref):
    rows, total = out_ref.shape[0], in_ref.shape[0]
    row = lax.broadcasted_iota(jnp.int32, (rows, total), 0)
    at = lax.broadcasted_iota(jnp.int32, (rows, total), 1)
    pick = jnp.where(lax.rem(at, rows) == row, 1.0, 0.0).astype(BF16)
    out_ref[...] = dot_nn(pick, in_ref[...])


def exchanged(array, axes):
    return lax.all_to_all(array, axes, split_axis=0, concat_axis=0, tiled=True)


def swapped(array):
    return lax.ppermute(array, CORE, [(0, 1), (1, 0)])


def on_device(tokens, router, w_in, w_out, grad_out):
    peers = lax.axis_size(SEQ)
    width = tokens.shape[2]
    row = 4 * width + LANES
    chips = lax.axis_size(CHIPS_EXP)
    tok, tok_t, grad, router_t, terms, mixing, mix, local, keep, send = run_first_pass(tokens, router, grad_out)
    recv = swapped(send)
    small = params(16)
    grad_t = pl.pallas_call(
        turn,
        in_specs=[VMEM],
        out_specs=VMEM,
        out_shape=jax.ShapeDtypeStruct(tok_t.shape, BF16),
        compiler_params=small,
        name="turn",
    )(grad)
    recv, grad_t = lax.optimization_barrier((recv, grad_t))
    halves = pl.pallas_call(
        merge_cores, out_shape=jax.ShapeDtypeStruct((chips, GROUP, row), BF16), compiler_params=small, name="merge_cores"
    )(keep, recv)
    column = pl.pallas_call(
        merge_column, out_shape=jax.ShapeDtypeStruct((peers, GROUP, row), BF16), compiler_params=small, name="merge_column"
    )(exchanged(halves, CHIPS_EXP))
    parts, rows, grads, hidden, pre_grad, slot_in, stats = run_experts(exchanged(column, SEQ), w_in, w_out)
    arrived = exchanged(parts, SEQ)
    grad_w_in, grad_w_out = run_weight_grads(rows, grads, hidden, pre_grad, w_in.shape[0])
    results = pl.pallas_call(
        slot_results, out_shape=jax.ShapeDtypeStruct((chips, GROUP, row), BF16), compiler_params=small, name="slot_results"
    )(arrived, slot_in, stats)
    mine = exchanged(results, CHIPS_EXP)
    other = swapped(mine)
    own_outs, own_backs, *own = run_half_products(tok_t, grad_t, mine, tokens.shape[0])
    other, *own = lax.optimization_barrier((other, *own))
    other_outs, other_backs, weights, part = run_second_pass(tok, tok_t, grad_t, terms, mixing, local, own, other)
    devices = lax.axis_size(SEQ_EXP)
    arrived = exchanged(part.reshape(devices, width // devices, part.shape[1]), SEQ_EXP)
    mixed, grad_tokens = run_token_outputs(mix, weights, own_outs, other_outs, own_backs, other_backs, router_t)
    grad_router = pl.pallas_call(
        add_up, out_shape=jax.ShapeDtypeStruct(arrived.shape[1:], F32), compiler_params=small, name="add_up"
    )(arrived.reshape(width, part.shape[1]))
    return (mixed, grad_tokens, grad_router, grad_w_in, grad_w_out)


def solution(mesh):
    finer = Mesh(mesh.devices.reshape(2, 4, 2, 4, 2), SEQ_EXP)
    return jax.shard_map(
        on_device,
        mesh=finer,
        in_specs=(
            P(None, SEQ_EXP, None),
            P(),
            P(EXP, None, SEQ),
            P(EXP, SEQ, None),
            P(None, SEQ_EXP, None),
        ),
        out_specs=(
            P(None, SEQ_EXP, None),
            P(None, SEQ_EXP, None),
            P(SEQ_EXP, None),
            P(EXP, None, SEQ),
            P(EXP, SEQ, None),
        ),
        check_vma=False,
    )
```

```python
import functools

import jax
import jax.numpy as jnp
from jax import lax
from jax.experimental import pallas as pl
from jax.experimental.pallas import tpu as pltpu
from jax.sharding import Mesh
from jax.sharding import PartitionSpec as P

SEQ = ("seq_0", "seq_1")
EXP = ("exp_0", "exp_1", "exp_2")
CHIPS_EXP = ("exp_0", "exp_1")
CORE = "exp_2"
SEQ_EXP = SEQ + EXP

F32 = jnp.float32
BF16 = jnp.bfloat16
LANES = 128
GROUP = 8


def dot_nt(a, b):
    return lax.dot_general(a, b, (((1,), (1,)), ((), ())), preferred_element_type=F32)


def dot_nn(a, b):
    return lax.dot_general(a, b, (((1,), (0,)), ((), ())), preferred_element_type=F32)


def dot_tn(a, b):
    return lax.dot_general(a, b, (((0,), (0,)), ((), ())), preferred_element_type=F32)


def params(mib, grid_dims=0):
    kinds = ("arbitrary",) * grid_dims if grid_dims else None
    return pltpu.CompilerParams(vmem_limit_bytes=mib << 20, dimension_semantics=kinds)


def pieces(value, count):
    found = []
    for _ in range(count):
        part = value.astype(BF16).astype(F32)
        found.append(part)
        value = value - part
    return found


def packed(columns):
    rows = columns[0].shape[0]
    lane = lax.broadcasted_iota(jnp.int32, (rows, LANES), 1)
    tile = jnp.zeros((rows, LANES), F32)
    for k, column in enumerate(columns):
        tile = jnp.where(lane == k, column, tile)
    return tile


def mixing_of(logits_t):
    peak = jnp.max(logits_t, axis=0, keepdims=True)
    terms = jnp.exp(logits_t - peak)
    return terms * (1.0 / jnp.sum(terms, axis=0, keepdims=True))


def first_pass(
    tok_hbm, router_hbm, grad_hbm, w_out_hbm,
    tok_ref, tok_t_ref, grad_ref, router_t_ref, terms_ref, mixing_ref, mix_ref, stats_ref, keep_ref, send_ref, w_out_ref,
    router_buf, router_f, sems,
):
    core = lax.axis_index(CORE)
    clips, rows, width = tok_ref.shape
    slots = router_t_ref.shape[0]
    half = slots // 2
    copies = [pltpu.make_async_copy(router_hbm, router_buf, sems.at[0])]
    for c in range(clips):
        copies.append(pltpu.make_async_copy(tok_hbm.at[c], tok_ref.at[c], sems.at[1 + c]))
    for c in range(clips):
        copies.append(pltpu.make_async_copy(grad_hbm.at[c], grad_ref.at[c], sems.at[1 + clips + c]))
    copies.append(pltpu.make_async_copy(w_out_hbm, w_out_ref, sems.at[1 + 2 * clips]))
    for copy in copies:
        copy.start()
    copies[0].wait()
    router_f[...] = router_buf[...].T.astype(F32)
    for k in range(slots // GROUP):
        place = k % (half // GROUP)
        side = core if k < half // GROUP else 1 - core
        at = pl.ds(pl.multiple_of((2 * place + side) * GROUP, GROUP), GROUP)
        router_t_ref[pl.ds(k * GROUP, GROUP), :] = router_f[at, :].astype(BF16)
    columns = [None] * 12
    for c in range(clips):
        copies[1 + c].wait()
        tok_t_ref[:, pl.ds(c * rows, rows)] = tok_ref[c].T
    both = dot_nn(router_t_ref[...], tok_t_ref[...])
    for c in range(clips):
        logits_t = both[:, c * rows : (c + 1) * rows]
        peak = jnp.max(logits_t, axis=1, keepdims=True)
        terms = jnp.exp(logits_t - peak)
        terms_ref[c] = terms
        mass = jnp.sum(terms, axis=1, keepdims=True)
        columns[3 * c : 3 * c + 3] = pieces(peak, 3)
        columns[6 + 3 * c : 9 + 3 * c] = pieces(mass, 3)
        sums = dot_nn(terms.astype(BF16), tok_ref[c]).astype(BF16)
        mixing = mixing_of(logits_t)
        mixing_ref[c] = mixing
        mix_ref[c] = mixing.astype(BF16)
        for q in range(keep_ref.shape[0]):
            at = pl.ds(c * width, width)
            keep_ref[q, :, at] = sums[q * GROUP : (q + 1) * GROUP]
            send_ref[q, :, at] = sums[half + q * GROUP : half + (q + 1) * GROUP]
    for c in range(clips):
        copies[1 + clips + c].wait()
    stats = packed(columns)
    stats_ref[...] = stats
    stats = stats.astype(BF16)
    for q in range(keep_ref.shape[0]):
        at = pl.ds(4 * width, LANES)
        keep_ref[q, :, at] = stats[q * GROUP : (q + 1) * GROUP]
        send_ref[q, :, at] = stats[half + q * GROUP : half + (q + 1) * GROUP]
    for c in range(clips):
        sums = dot_nn(mix_ref[c], grad_ref[c]).astype(BF16)
        for q in range(keep_ref.shape[0]):
            at = pl.ds((2 + c) * width, width)
            keep_ref[q, :, at] = sums[q * GROUP : (q + 1) * GROUP]
            send_ref[q, :, at] = sums[half + q * GROUP : half + (q + 1) * GROUP]
    copies[1 + 2 * clips].wait()


VMEM = pl.BlockSpec(memory_space=pltpu.VMEM)
HBM = pl.BlockSpec(memory_space=pltpu.HBM)


def run_first_pass(tokens, router, grad_out, w_out):
    clips, rows, width = tokens.shape
    slots = router.shape[1]
    row = 4 * width + LANES
    groups = slots // GROUP // 2
    shapes = [
        (tokens.shape, BF16),
        ((width, clips * rows), BF16),
        (grad_out.shape, BF16),
        ((slots, width), BF16),
        ((clips, slots, rows), F32),
        ((clips, slots, rows), F32),
        ((clips, slots, rows), BF16),
        ((slots, LANES), F32),
        ((groups, GROUP, row), BF16),
        ((groups, GROUP, row), BF16),
        (w_out.shape, BF16),
    ]
    return pl.pallas_call(
        first_pass,
        in_specs=[HBM] * 4,
        out_specs=[VMEM] * len(shapes),
        out_shape=[jax.ShapeDtypeStruct(*shape) for shape in shapes],
        scratch_shapes=[
            pltpu.VMEM(router.shape, BF16),
            pltpu.VMEM((slots, width), F32),
            pltpu.SemaphoreType.DMA((2 + 2 * clips,)),
        ],
        compiler_params=params(28),
        name="first_pass",
    )(*(pltpu.with_memory_space_constraint(a, pltpu.HBM) for a in (tokens, router, grad_out, w_out)))


def whole_of(tile, at):
    return tile[:, at : at + 1] + tile[:, at + 1 : at + 2] + tile[:, at + 2 : at + 3]


def merged(blocks, width):
    tiles = [load(4 * width, LANES) for load in blocks]
    inputs, grads, peaks, masses = [], [], [], []
    for c in range(2):
        tops = [whole_of(tile, 3 * c) for tile in tiles]
        peaks.append(functools.reduce(jnp.maximum, tops))
        columns = [jnp.exp(top - peaks[c]) for top in tops]
        masses.append(sum(col * whole_of(tile, 6 + 3 * c) for col, tile in zip(columns, tiles)))
        inputs.append(sum(col * load(c * width, width) for col, load in zip(columns, blocks)))
        grads.append(sum(load((2 + c) * width, width) for load in blocks))
    return inputs, grads, peaks, masses


def loader(ref, index):
    return lambda at, size: ref[index, :, pl.ds(at, size)].astype(F32)


def stat_tile(peaks, masses):
    return packed([piece for value in (*peaks, *masses) for piece in pieces(value, 3)])


def merge_cores(keep_ref, recv_ref, out_ref):
    width = (keep_ref.shape[2] - LANES) // 4
    for q in range(keep_ref.shape[0]):
        inputs, grads, peaks, masses = merged([loader(keep_ref, q), loader(recv_ref, q)], width)
        for k, value in enumerate(inputs + grads):
            out_ref[q, :, pl.ds(k * width, width)] = value.astype(BF16)
        out_ref[q, :, pl.ds(4 * width, LANES)] = stat_tile(peaks, masses).astype(BF16)


def merge_column(in_ref, out_ref):
    width = (in_ref.shape[2] - LANES) // 4
    blocks = [loader(in_ref, k) for k in range(in_ref.shape[0])]
    inputs, grads, peaks, masses = merged(blocks, width)
    for k, value in enumerate(inputs + grads):
        for q in range(out_ref.shape[0]):
            out_ref[q, :, pl.ds(k * width, width)] = value.astype(BF16)
    for q in range(out_ref.shape[0]):
        out_ref[q, :, pl.ds(4 * width, LANES)] = stat_tile(peaks, masses).astype(BF16)


GELU_A = 0.7978845608028654
GELU_B = 0.044715


def experts(
    in_ref, w_in_ref, w_out_ref, w_out_t_ref,
    out_ref, rows_ref, grads_ref, hidden_ref, pre_grad_ref, slot_in_ref, stats_ref,
):
    width = w_in_ref.shape[1]
    count = w_in_ref.shape[0]
    blocks = [loader(in_ref, k) for k in range(in_ref.shape[0])]
    inputs, grads, peaks, masses = merged(blocks, width)
    slot_in = jnp.concatenate([value / mass for value, mass in zip(inputs, masses)], axis=0)
    slot_in_ref[...] = slot_in
    stats_ref[...] = stat_tile(peaks, masses)
    x = slot_in.astype(BF16)
    g = jnp.concatenate(grads, axis=0).astype(BF16)
    rows_ref[...] = x
    grads_ref[...] = g
    total = x.shape[0]
    hid = w_in_ref.shape[2]
    owner = lambda shape: lax.rem(lax.broadcasted_iota(jnp.int32, shape, 0), GROUP) // (GROUP // count)
    who = owner((total, hid))
    pre = jnp.zeros((total, hid), F32)
    hidden_grad = jnp.zeros((total, hid), F32)
    for e in range(count):
        pre = jnp.where(who == e, dot_nn(x, w_in_ref[e]), pre)
        hidden_grad = jnp.where(who == e, dot_nn(g, w_out_t_ref[e]), hidden_grad)
    inner = jnp.tanh(GELU_A * (pre + GELU_B * pre * pre * pre))
    hidden = 0.5 * pre * (1.0 + inner)
    slope = 0.5 * (1.0 + inner) + 0.5 * pre * (1.0 - inner * inner) * GELU_A * (1.0 + 3.0 * GELU_B * pre * pre)
    pre_grad = hidden_grad * slope
    hidden_ref[...] = hidden.astype(BF16)
    pre_grad_ref[...] = pre_grad.astype(BF16)
    out_part = jnp.zeros((total, width), F32)
    in_part = jnp.zeros((total, width), F32)
    for e in range(count):
        out_part += dot_nn(jnp.where(who == e, hidden, 0.0).astype(BF16), w_out_ref[e])
        in_part += dot_nt(jnp.where(who == e, pre_grad, 0.0).astype(BF16), w_in_ref[e])
    both = jnp.concatenate([out_part, in_part], axis=0).astype(BF16)
    for q in range(out_ref.shape[0]):
        out_ref[q] = both


def run_experts(sums, w_in, w_out, w_out_t):
    count, width, hid = w_in.shape
    peers = sums.shape[0]
    rows = 2 * GROUP
    return pl.pallas_call(
        experts,
        out_shape=[
            jax.ShapeDtypeStruct((peers, 2 * rows, width), BF16),
            jax.ShapeDtypeStruct((rows, width), BF16),
            jax.ShapeDtypeStruct((rows, width), BF16),
            jax.ShapeDtypeStruct((rows, hid), BF16),
            jax.ShapeDtypeStruct((rows, hid), BF16),
            jax.ShapeDtypeStruct((rows, width), F32),
            jax.ShapeDtypeStruct((GROUP, LANES), F32),
        ],
        compiler_params=params(16),
        name="experts",
    )(sums, w_in, w_out, w_out_t)


def weight_grads(rows_ref, grads_ref, hidden_ref, pre_grad_ref, w_in_grad_ref, w_out_grad_ref):
    e = pl.program_id(0)
    total, hid = hidden_ref.shape
    count = pl.num_programs(0)
    who = lax.rem(lax.broadcasted_iota(jnp.int32, (total, hid), 0), GROUP) // (GROUP // 2)
    mask = who == e
    hidden = jnp.where(mask, hidden_ref[...].astype(F32), 0.0).astype(BF16)
    pre_grad = jnp.where(mask, pre_grad_ref[...].astype(F32), 0.0).astype(BF16)
    w_out_grad_ref[0] = dot_tn(hidden, grads_ref[...]).astype(BF16)
    w_in_grad_ref[0] = dot_tn(rows_ref[...], pre_grad).astype(BF16)


def run_weight_grads(rows, grads, hidden, pre_grad, count):
    total, width = rows.shape
    hid = hidden.shape[1]
    whole = lambda *shape: pl.BlockSpec(shape, lambda e: (0,) * len(shape))
    return pl.pallas_call(
        weight_grads,
        grid=(count,),
        in_specs=[whole(total, width), whole(total, width), whole(total, hid), whole(total, hid)],
        out_specs=[
            pl.BlockSpec((1, width, hid), lambda e: (e, 0, 0)),
            pl.BlockSpec((1, hid, width), lambda e: (e, 0, 0)),
        ],
        out_shape=[
            jax.ShapeDtypeStruct((count, width, hid), BF16),
            jax.ShapeDtypeStruct((count, hid, width), BF16),
        ],
        compiler_params=params(16, 1),
        cost_estimate=pl.CostEstimate(
            flops=4 * count * total * width * hid, transcendentals=0, bytes_accessed=4 * count * width * hid
        ),
        name="weight_grads",
    )(rows, grads, hidden, pre_grad)


def slot_results(in_ref, slot_in_ref, stats_ref, out_ref):
    width = in_ref.shape[2]
    total = sum(in_ref[k].astype(F32) for k in range(in_ref.shape[0])).astype(BF16)
    back = total[2 * GROUP :].astype(F32)
    inner = jnp.sum(back * slot_in_ref[...], axis=1, keepdims=True)
    tile = stats_ref[...]
    lane = lax.broadcasted_iota(jnp.int32, tile.shape, 1)
    for c in range(2):
        for k, column in enumerate(pieces(inner[c * GROUP : (c + 1) * GROUP], 3)):
            tile = jnp.where(lane == 12 + 3 * c + k, column, tile)
    for q in range(out_ref.shape[0]):
        for k in range(4):
            out_ref[q, :, pl.ds(k * width, width)] = total[k * GROUP : (k + 1) * GROUP]
        out_ref[q, :, pl.ds(4 * width, LANES)] = tile.astype(BF16)


def turn(grad_ref, w_out_ref, grad_t_ref, w_out_t_ref):
    rows = grad_ref.shape[1]
    for c in range(grad_ref.shape[0]):
        grad_t_ref[:, pl.ds(c * rows, rows)] = grad_ref[c].T
    for e in range(w_out_ref.shape[0]):
        w_out_t_ref[e] = w_out_ref[e].T


def run_turn(grad, w_out):
    clips, rows, width = grad.shape
    shapes = [(width, clips * rows), (w_out.shape[0], width, w_out.shape[1])]
    return pl.pallas_call(
        turn,
        in_specs=[VMEM] * 2,
        out_specs=[VMEM] * len(shapes),
        out_shape=[jax.ShapeDtypeStruct(shape, BF16) for shape in shapes],
        compiler_params=params(16),
        name="turn",
    )(grad, w_out)


def half_products(tok_t_ref, grad_t_ref, slots_ref, outs_ref, backs_ref, stats_ref, dispatch_grad_ref, mixing_grad_ref):
    clips, rows = outs_ref.shape[0], dispatch_grad_ref.shape[2]
    width = outs_ref.shape[2]
    for q in range(slots_ref.shape[0]):
        at = pl.ds(q * GROUP, GROUP)
        for c in range(clips):
            outs_ref[c, at, :] = slots_ref[q, :, pl.ds(c * width, width)]
            backs_ref[c, at, :] = slots_ref[q, :, pl.ds((2 + c) * width, width)]
        stats_ref[at, :] = slots_ref[q, :, pl.ds(4 * width, LANES)].astype(F32)
    for c in range(clips):
        at = pl.ds(c * rows, rows)
        dispatch_grad_ref[c] = dot_nn(backs_ref[c], tok_t_ref[:, at])
        mixing_grad_ref[c] = dot_nn(outs_ref[c], grad_t_ref[:, at])


def run_half_products(tok_t, grad_t, slots, clips):
    half, width = slots.shape[0] * GROUP, tok_t.shape[0]
    rows = tok_t.shape[1] // clips
    shapes = [
        ((clips, half, width), BF16),
        ((clips, half, width), BF16),
        ((half, LANES), F32),
        ((clips, half, rows), F32),
        ((clips, half, rows), F32),
    ]
    return pl.pallas_call(
        half_products,
        in_specs=[VMEM] * 3,
        out_specs=[VMEM] * len(shapes),
        out_shape=[jax.ShapeDtypeStruct(*shape) for shape in shapes],
        compiler_params=params(16),
        name="half_products",
    )(tok_t, grad_t, slots)


def second_pass(
    tok_ref, tok_t_ref, grad_t_ref, terms_ref, mixing_ref, local_ref,
    own_stats_ref, own_dispatch_ref, own_mixing_ref, slots_ref,
    outs_ref, backs_ref, weights_ref, part_ref, stats_ref, other_dispatch_ref, other_mixing_ref, ordered,
):
    core = lax.axis_index(CORE)
    clips, rows, width = tok_ref.shape
    slots = terms_ref.shape[1]
    half = slots // 2
    half_products(
        tok_t_ref, grad_t_ref, slots_ref, outs_ref, backs_ref, stats_ref, other_dispatch_ref, other_mixing_ref
    )
    tile = jnp.concatenate([own_stats_ref[...], stats_ref[...]], axis=0)
    local = local_ref[...]
    total = jnp.zeros((slots, width), F32)
    for c in range(clips):
        mass, inner = whole_of(tile, 6 + 3 * c), whole_of(tile, 12 + 3 * c)
        scale = jnp.exp(whole_of(local, 3 * c) - whole_of(tile, 3 * c)) / mass
        dispatch = terms_ref[c] * scale
        weights_ref[c, pl.ds(0, slots), :] = dispatch.astype(BF16)
        mixing = mixing_ref[c]
        dispatch_grad = jnp.concatenate([own_dispatch_ref[c], other_dispatch_ref[c]], axis=0)
        mixing_grad = jnp.concatenate([own_mixing_ref[c], other_mixing_ref[c]], axis=0)
        logit_grad = dispatch * (dispatch_grad - inner) + mixing * (
            mixing_grad - jnp.sum(mixing * mixing_grad, axis=0, keepdims=True)
        )
        logit_b = logit_grad.astype(BF16)
        weights_ref[c, pl.ds(slots, slots), :] = logit_b
        total = total + dot_nn(logit_b, tok_ref[c])
    for k in range(slots // GROUP):
        place = k % (half // GROUP)
        side = core if k < half // GROUP else 1 - core
        at = pl.ds(pl.multiple_of((2 * place + side) * GROUP, GROUP), GROUP)
        ordered[at, :] = total[k * GROUP : (k + 1) * GROUP]
    part_ref[...] = ordered[...].T.astype(BF16)


def run_second_pass(tok, tok_t, grad_t, terms, mixing, local, own, other):
    clips, rows, width = tok.shape
    slots = terms.shape[1]
    shapes = [(clips, slots // 2, width), (clips, slots // 2, width), (clips, 2 * slots, rows), (width, slots)]
    return pl.pallas_call(
        second_pass,
        in_specs=[VMEM] * 10,
        out_specs=[VMEM] * len(shapes),
        out_shape=[jax.ShapeDtypeStruct(shape, BF16) for shape in shapes],
        scratch_shapes=[
            pltpu.VMEM((slots // 2, LANES), F32),
            pltpu.VMEM((clips, slots // 2, rows), F32),
            pltpu.VMEM((clips, slots // 2, rows), F32),
            pltpu.VMEM((slots, width), F32),
        ],
        compiler_params=params(24),
        name="second_pass",
    )(tok, tok_t, grad_t, terms, mixing, local, *own, other)


def token_outputs(
    mix_ref, weights_ref, own_outs_ref, other_outs_ref, own_backs_ref, other_backs_ref, router_t_ref,
    mixed_ref, grad_tokens_ref,
):
    outs = jnp.concatenate([own_outs_ref[0], other_outs_ref[0]], axis=0)
    backs = jnp.concatenate([own_backs_ref[0], other_backs_ref[0], router_t_ref[...]], axis=0)
    mixed_ref[0] = dot_tn(mix_ref[0], outs).astype(BF16)
    grad_tokens_ref[0] = dot_tn(weights_ref[0], backs).astype(BF16)


def run_token_outputs(mix, weights, own_outs, other_outs, own_backs, other_backs, router_t):
    clips, slots, rows = mix.shape
    width = own_outs.shape[2]
    block = 384
    out = pl.BlockSpec((1, block, width), lambda c, t: (c, t, 0))
    part = pl.BlockSpec((1, slots // 2, width), lambda c, t: (c, 0, 0))
    return pl.pallas_call(
        token_outputs,
        grid=(clips, rows // block),
        in_specs=[
            pl.BlockSpec((1, slots, block), lambda c, t: (c, 0, t)),
            pl.BlockSpec((1, 2 * slots, block), lambda c, t: (c, 0, t)),
            part,
            part,
            part,
            part,
            pl.BlockSpec((slots, width), lambda c, t: (0, 0)),
        ],
        out_specs=[out, out],
        out_shape=[jax.ShapeDtypeStruct((clips, rows, width), BF16)] * 2,
        compiler_params=params(16, 2),
        cost_estimate=pl.CostEstimate(
            flops=6 * clips * rows * slots * width, transcendentals=0, bytes_accessed=6 * clips * rows * width
        ),
        name="token_outputs",
    )(mix, weights, own_outs, other_outs, own_backs, other_backs, router_t)


def add_up(in_ref, out_ref):
    rows, total = out_ref.shape[0], in_ref.shape[0]
    row = lax.broadcasted_iota(jnp.int32, (rows, total), 0)
    at = lax.broadcasted_iota(jnp.int32, (rows, total), 1)
    pick = jnp.where(lax.rem(at, rows) == row, 1.0, 0.0).astype(BF16)
    out_ref[...] = dot_nn(pick, in_ref[...])


def exchanged(array, axes):
    return lax.all_to_all(array, axes, split_axis=0, concat_axis=0, tiled=True)


def swapped(array):
    return lax.ppermute(array, CORE, [(0, 1), (1, 0)])


def on_device(tokens, router, w_in, w_out, grad_out):
    peers = lax.axis_size(SEQ)
    width = tokens.shape[2]
    row = 4 * width + LANES
    chips = lax.axis_size(CHIPS_EXP)
    tok, tok_t, grad, router_t, terms, mixing, mix, local, keep, send, w_out = run_first_pass(
        tokens, router, grad_out, w_out
    )
    recv = swapped(send)
    small = params(16)
    grad_t, w_out_t = run_turn(grad, w_out)
    recv, grad_t, w_out_t = lax.optimization_barrier((recv, grad_t, w_out_t))
    halves = pl.pallas_call(
        merge_cores, out_shape=jax.ShapeDtypeStruct((chips, GROUP, row), BF16), compiler_params=small, name="merge_cores"
    )(keep, recv)
    column = pl.pallas_call(
        merge_column, out_shape=jax.ShapeDtypeStruct((peers, GROUP, row), BF16), compiler_params=small, name="merge_column"
    )(exchanged(halves, CHIPS_EXP))
    parts, rows, grads, hidden, pre_grad, slot_in, stats = run_experts(
        exchanged(column, SEQ), w_in, w_out, w_out_t
    )
    arrived = exchanged(parts, SEQ)
    grad_w_in, grad_w_out = run_weight_grads(rows, grads, hidden, pre_grad, w_in.shape[0])
    results = pl.pallas_call(
        slot_results, out_shape=jax.ShapeDtypeStruct((chips, GROUP, row), BF16), compiler_params=small, name="slot_results"
    )(arrived, slot_in, stats)
    mine = exchanged(results, CHIPS_EXP)
    other = swapped(mine)
    own_outs, own_backs, *own = run_half_products(tok_t, grad_t, mine, tokens.shape[0])
    other, *own = lax.optimization_barrier((other, *own))
    other_outs, other_backs, weights, part = run_second_pass(tok, tok_t, grad_t, terms, mixing, local, own, other)
    devices = lax.axis_size(SEQ_EXP)
    arrived = exchanged(part.reshape(devices, width // devices, part.shape[1]), SEQ_EXP)
    mixed, grad_tokens = run_token_outputs(mix, weights, own_outs, other_outs, own_backs, other_backs, router_t)
    grad_router = pl.pallas_call(
        add_up, out_shape=jax.ShapeDtypeStruct(arrived.shape[1:], F32), compiler_params=small, name="add_up"
    )(arrived.reshape(width, part.shape[1]))
    return (mixed, grad_tokens, grad_router, grad_w_in, grad_w_out)


def solution(mesh):
    finer = Mesh(mesh.devices.reshape(2, 4, 2, 4, 2), SEQ_EXP)
    return jax.shard_map(
        on_device,
        mesh=finer,
        in_specs=(
            P(None, SEQ_EXP, None),
            P(),
            P(EXP, None, SEQ),
            P(EXP, SEQ, None),
            P(None, SEQ_EXP, None),
        ),
        out_specs=(
            P(None, SEQ_EXP, None),
            P(None, SEQ_EXP, None),
            P(SEQ_EXP, None),
            P(EXP, None, SEQ),
            P(EXP, SEQ, None),
        ),
        check_vma=False,
    )
```
